512 devices in a mesh: ctx: 32 (over z_lo, x), tp: 16 (over y, z_hi, core).
Axes of the slice: x: 4, y: 4, z: 16 (z_hi: 2, z_lo: 8; z = z_hi * 8 + z_lo), core: 2. Of those that a mesh axis runs over, the one named last changes fastest.
Arguments:
- query_plain: bfloat16 [4096, 8192], P('ctx', 'tp'), may hold values from -6 to 6
- query_rotary: bfloat16 [4096, 4096], P('ctx', 'tp'), may hold values from -6 to 6
- latent_keys: bfloat16 [4096, 576], P(('ctx', 'tp')), may hold values from -100 to 100
- span_order: int32 [64], replicated, may hold values from 0 to 63, each once
- key_up: bfloat16 [64, 128, 512], P('tp'), may hold values from -0.5 to 0.5
- value_up: bfloat16 [64, 512, 128], P('tp'), may hold values from -0.5 to 0.5
- output_weight: bfloat16 [8192, 3584], P('tp'), may hold values from -0.125 to 0.125
Outputs:
- mixed: bfloat16 [4096, 3584], P('ctx', 'tp')
The draws below stay inside these ranges and needn't reach their ends.
Inputs may be any that keep to these rules, and one draw needn't show every extreme that they name: Stored rows s * 64 to (s + 1) * 64 - 1 are the tokens of span span_order[s] of the sequence, in order; each span appears once.
All inputs are finite; a program needn't handle non-finite values.
Results may differ from the reference program's by a relative error of at most 0.015.
Values may be sent and summed in bfloat16 or wider, within the bound.
No kernel may reach another device: no remote copies, remote signals or barrier semaphores. Data moves between devices by JAX's collectives and lax.ppermute only.
A program may use at most 64 MiB of HBM per device.

```python
import math
import jax
import jax.numpy as jnp
from jax import lax

D = 3584
H = 64
NOPE = 128
ROPE = 64
LAT = 512
VD = 128
TOKENS = 4096
SPAN = 64
NCHUNK = 64


def draw_latent_keys(key, part):
    array_shape = (TOKENS, LAT + ROPE)
    values = jax.random.normal(jax.random.fold_in(key, 7), array_shape, jnp.float32)
    return jnp.clip(values, -6.0, 6.0).astype(jnp.bfloat16)


def block_levels(own_key, shape, cuts, smallest, high):
    def one(position, blocks):
        heights = jax.random.uniform(jax.random.fold_in(jax.random.fold_in(own_key, 6), position), (blocks,), jnp.float32, smallest / len(cuts), high / len(cuts))
        return jnp.repeat(jnp.exp(heights), shape[position] // blocks).reshape((-1,) + (1,) * (len(shape) - position - 1))

    factor_of = one(*cuts[0])
    for cut in cuts[1:]:
        factor_of = factor_of * one(*cut)
    return factor_of


def noise(key, shape, scale, reach, cuts=(), kind=jnp.bfloat16):
    result = scale * jax.random.normal(key, shape, jnp.float32)
    if cuts:
        result = result * block_levels(key, shape, cuts, -0.22, 0.18)
    return jnp.clip(result, -reach, reach).astype(kind)


def setup_inputs(seed: int = 0) -> dict:
    key_of = jax.random.split(jax.random.key(seed), 8)
    return {
        "query_plain": noise(key_of[0], (TOKENS, H * NOPE), 1.0, 6.0, ((0, 32), (1, 16))),
        "query_rotary": noise(key_of[1], (TOKENS, H * ROPE), 1.0, 6.0, ((0, 32), (1, 16))),
        "latent_keys": draw_latent_keys(jax.random.fold_in(key_of[7], 71), 0),
        "span_order": jax.random.permutation(key_of[3], NCHUNK).astype(jnp.int32),
        "key_up": noise(key_of[4], (H, NOPE, LAT), NOPE ** -0.5, 0.5, ((0, 16),)),
        "value_up": noise(key_of[5], (H, LAT, VD), (LAT // 4) ** -0.5, 0.5, ((0, 16),)),
        "output_weight": noise(key_of[6], (H * VD, D), (H * VD // 4) ** -0.5, 0.125, ((0, 16),)),
    }


rope_base = 10000.0

def rotate_pairs(values, places):
    halfway = values.shape[-1] // 2
    frequency = rope_base ** (-jnp.arange(halfway, dtype=jnp.float32) * 2.0 / values.shape[-1])
    angles = places.astype(jnp.float32)[:, None] * frequency[None, :]
    cosine = jnp.cos(angles)
    sine_part = jnp.sin(angles)
    first_half = values[..., :halfway]
    second_half = values[..., halfway:]
    return jnp.concatenate([first_half * cosine - second_half * sine_part, first_half * sine_part + second_half * cosine], axis=-1)

def reference(query_plain, query_rotary, latent_keys, span_order, key_up, value_up, output_weight):
    row_ids = jnp.arange(TOKENS, dtype=jnp.int32)
    places = (span_order[row_ids // SPAN] * SPAN + row_ids % SPAN).astype(jnp.int32)
    latent = latent_keys[:, :LAT]
    turned_keys = rotate_pairs(latent_keys[:, LAT:].astype(jnp.float32), places).astype(jnp.bfloat16)
    all_keys = jnp.concatenate([latent, turned_keys], axis=1)
    allowed = places[None, :] <= places[:, None]
    score_scale = 1.0 / math.sqrt(NOPE + ROPE)
    plain_heads = jnp.swapaxes(query_plain.reshape(TOKENS, H, NOPE), 0, 1)
    rotary_heads = jnp.swapaxes(query_rotary.reshape(TOKENS, H, ROPE), 0, 1)

    def one_head(inputs):
        head_plain, head_rotary, head_key_up, head_value_up = inputs
        absorbed = jnp.dot(head_plain, head_key_up, preferred_element_type=jnp.float32).astype(jnp.bfloat16)
        turned = rotate_pairs(head_rotary.astype(jnp.float32), places).astype(jnp.bfloat16)
        head_queries = jnp.concatenate([absorbed, turned], axis=1)
        scores = jnp.dot(head_queries, all_keys.T, preferred_element_type=jnp.float32) * score_scale
        highest = lax.optimization_barrier(jnp.max(jnp.where(allowed, scores, -jnp.inf), axis=1, keepdims=True))
        raised = jnp.where(allowed, jnp.exp(scores - highest), 0.0)
        weights = raised.astype(jnp.bfloat16)
        context = jnp.dot(weights, latent, preferred_element_type=jnp.float32) / lax.optimization_barrier(jnp.sum(raised, axis=1, keepdims=True))
        context = context.astype(jnp.bfloat16)
        return jnp.dot(context, head_value_up, preferred_element_type=jnp.float32).astype(jnp.bfloat16)
    head_out = lax.map(one_head, (plain_heads, rotary_heads, key_up, value_up))
    flat_out = jnp.swapaxes(head_out, 0, 1).reshape(TOKENS, H * VD)
    return jnp.dot(flat_out, output_weight, preferred_element_type=jnp.float32).astype(jnp.bfloat16)
```

```python
import functools
import math

import jax
import jax.numpy as jnp
import numpy as np
from jax import lax
from jax.experimental import pallas as pl
from jax.experimental.pallas import tpu as pltpu
from jax.sharding import Mesh
from jax.sharding import PartitionSpec as P

NZL, NX, NY, NZH, NC = 8, 4, 4, 2, 2
CTX = ("zl", "x")
TP = ("y", "zh", "c")

SPAN = 64
ROPE = 64
LAT = 512
NOPE = 128
VD = 128
HEADS = 4
KEYW = LAT + ROPE
QW = HEADS * (NOPE + ROPE)
OUTW = HEADS * VD + 128
BASE = 10000.0
LOW = -1e30
VMEM_LIMIT = 48 * 1024 * 1024


def rotary_tables():
    lane = np.arange(128)
    freq = BASE ** (-2.0 * (lane % 32) / ROPE)
    sign = np.where(lane % 64 < 32, -1.0, 1.0)
    start = (np.arange(64) * SPAN)[:, None] * freq[None, :]
    offset = np.arange(SPAN)[:, None] * freq[None, :]
    tables = [np.cos(start), sign * np.sin(start), np.cos(offset), sign * np.sin(offset)]
    return np.stack(tables).astype(np.float32)


def turn(values, cosine, signed_sine):
    lane = lax.broadcasted_iota(jnp.int32, values.shape, 1)
    partner = jnp.where(
        lane % 64 < 32, pltpu.roll(values, 96, axis=1), pltpu.roll(values, 32, axis=1)
    )
    return values * cosine + partner * signed_sine


def angle_of(tables_ref, span, offset_rows):
    cos_a = tables_ref[0, pl.ds(span, 1), :]
    sin_a = tables_ref[1, pl.ds(span, 1), :]
    cos_b = tables_ref[2, offset_rows, :]
    sin_b = tables_ref[3, offset_rows, :]
    return cos_a * cos_b - sin_a * sin_b, sin_a * cos_b + cos_a * sin_b


def prepare_kernel(where_ref, spans_ref, plain_ref, rotary_ref, keys_ref, tables_ref, kb_ref, q_ref):
    ctx = where_ref[0]
    tp = where_ref[1]
    own_span = spans_ref[ctx * 2 + tp // 8]
    first = pl.multiple_of((tp % 8) * 8, 8)
    cosine, sine = angle_of(tables_ref, own_span, pl.ds(first, 8))
    tail = keys_ref[:, LAT:].astype(jnp.float32)
    turned = turn(jnp.concatenate([tail, tail], axis=1), cosine, sine).astype(jnp.bfloat16)
    for k in range(kb_ref.shape[0]):
        kb_ref[k, :, :LAT] = keys_ref[:, :LAT]
        kb_ref[k, :, LAT:] = turned[:, :ROPE]
    q_ref[:, : HEADS * NOPE] = plain_ref[...]
    for s in range(2):
        cosine, sine = angle_of(tables_ref, spans_ref[ctx * 2 + s], pl.ds(0, SPAN))
        for j in range(HEADS * ROPE // 128):
            part = rotary_ref[s * SPAN : (s + 1) * SPAN, j * 128 : (j + 1) * 128]
            q_ref[s * SPAN : (s + 1) * SPAN, HEADS * NOPE + j * 128 : HEADS * NOPE + (j + 1) * 128] = turn(
                part.astype(jnp.float32), cosine, sine
            ).astype(jnp.bfloat16)


def prepare(where, spans, plain, rotary, keys):
    smem = pl.BlockSpec(memory_space=pltpu.SMEM)
    vmem = pl.BlockSpec(memory_space=pltpu.VMEM)
    return pl.pallas_call(
        prepare_kernel,
        out_shape=(
            jax.ShapeDtypeStruct((NZL * NZH, 8, KEYW), jnp.bfloat16),
            jax.ShapeDtypeStruct((2 * SPAN, QW), jnp.bfloat16),
        ),
        in_specs=[smem, smem, vmem, vmem, vmem, vmem],
        out_specs=(vmem, vmem),
    )(where, spans, plain, rotary, keys, jnp.asarray(rotary_tables()))


def attend_kernel(
    where_ref, spans_ref, q0, q1, q2, q3, own_ref, other_ref, kp_own_ref, kp_other_ref, up_ref, value_ref, out_ref, query
):
    zl = where_ref[0] // NX
    x = where_ref[0] % NX
    scale = math.log2(math.e) / math.sqrt(NOPE + ROPE)
    for k, block in enumerate((q0, q1, q2, q3)):
        source = (x + NX - k) % NX
        for s in range(2):
            rows = slice(s * SPAN, (s + 1) * SPAN)
            for h in range(HEADS):
                at = slice(h * SPAN, (h + 1) * SPAN)
                query[at, :LAT] = jnp.dot(
                    block[rows, h * NOPE : (h + 1) * NOPE], up_ref[h], preferred_element_type=jnp.float32
                ).astype(jnp.bfloat16)
                query[at, LAT:] = block[rows, HEADS * NOPE + h * ROPE : HEADS * NOPE + (h + 1) * ROPE]
            place = spans_ref[(zl * NX + source) * 2 + s] * SPAN + (
                lax.broadcasted_iota(jnp.int32, (HEADS * SPAN, 1), 0) % SPAN
            )
            dims = (((1,), (1,)), ((), ()))
            scores = []
            for keys, key_place in ((own_ref, kp_own_ref), (other_ref, kp_other_ref)):
                raw = lax.dot_general(query[...], keys[...], dims, preferred_element_type=jnp.float32)
                scores.append(jnp.where(key_place[...] <= place, raw * scale, LOW))
            highest = jnp.maximum(
                jnp.max(scores[0], axis=1, keepdims=True), jnp.max(scores[1], axis=1, keepdims=True)
            )
            total = jnp.zeros((HEADS * SPAN, 1), jnp.float32)
            context = jnp.zeros((HEADS * SPAN, LAT), jnp.float32)
            for score, keys in zip(scores, (own_ref, other_ref)):
                raised = jnp.exp2(score - highest)
                total = total + jnp.sum(raised, axis=1, keepdims=True)
                context = context + jnp.dot(
                    raised.astype(jnp.bfloat16), keys[:, :LAT], preferred_element_type=jnp.float32
                )
            context = (context / total).astype(jnp.bfloat16)
            log_sum = highest + jnp.log2(total)
            high = log_sum.astype(jnp.bfloat16).astype(jnp.float32)
            rest = log_sum - high
            middle = rest.astype(jnp.bfloat16).astype(jnp.float32)
            low = rest - middle
            lane = lax.broadcasted_iota(jnp.int32, (SPAN, 128), 1)
            packed = jnp.zeros((SPAN, 128), jnp.float32)
            for h in range(HEADS):
                at = slice(h * SPAN, (h + 1) * SPAN)
                out_ref[source, rows, h * VD : (h + 1) * VD] = jnp.dot(
                    context[at], value_ref[h], preferred_element_type=jnp.float32
                ).astype(jnp.bfloat16)
                for n, part in enumerate((high, middle, low)):
                    packed = jnp.where(lane == n * HEADS + h, part[at], packed)
            out_ref[source, rows, HEADS * VD :] = packed.astype(jnp.bfloat16)


def attend(where, spans, blocks, own, other, places, key_up, value_up):
    smem = pl.BlockSpec(memory_space=pltpu.SMEM)
    vmem = pl.BlockSpec(memory_space=pltpu.VMEM)
    return pl.pallas_call(
        attend_kernel,
        out_shape=jax.ShapeDtypeStruct((NX, 2 * SPAN, OUTW), jnp.bfloat16),
        in_specs=[smem, smem] + [vmem] * 10,
        out_specs=vmem,
        scratch_shapes=[pltpu.VMEM((HEADS * SPAN, KEYW), jnp.bfloat16)],
        compiler_params=pltpu.CompilerParams(vmem_limit_bytes=VMEM_LIMIT),
    )(where, spans, *blocks, own, other, *places, key_up, value_up)


def project_kernel(where_ref, parts_ref, weight_ref, send_ref, keep_ref, head_out):
    c = where_ref[1] % NC

    @pl.when(pl.program_id(0) == 0)
    def _():
        packed = [parts_ref[i, :, HEADS * VD :].astype(jnp.float32) for i in range(NX)]
        for h in range(HEADS):
            logs = [
                (p[:, h : h + 1] + p[:, HEADS + h : HEADS + h + 1]) + p[:, 2 * HEADS + h : 2 * HEADS + h + 1]
                for p in packed
            ]
            highest = functools.reduce(jnp.maximum, logs)
            shares = [jnp.exp2(v - highest) for v in logs]
            total = functools.reduce(jnp.add, shares)
            merged = functools.reduce(
                jnp.add,
                [
                    shares[i] * parts_ref[i, :, h * VD : (h + 1) * VD].astype(jnp.float32)
                    for i in range(NX)
                ],
            )
            head_out[:, h * VD : (h + 1) * VD] = (merged / total).astype(jnp.bfloat16)

    result = jnp.dot(head_out[...], weight_ref[...], preferred_element_type=jnp.float32).astype(jnp.bfloat16)
    width = result.shape[1] // (NZH * NC)
    for zh in range(NZH):
        even = result[:, 2 * zh * width : (2 * zh + 1) * width]
        odd = result[:, (2 * zh + 1) * width : (2 * zh + 2) * width]
        keep_ref[0, zh] = jnp.where(c == 0, even, odd)
        send_ref[0, zh] = jnp.where(c == 0, odd, even)


def project(where, parts, weight):
    rows = parts.shape[1]
    columns = weight.shape[1]
    step = columns // NY
    width = step // (NZH * NC)
    piece = jax.ShapeDtypeStruct((NY, NZH, rows, width), jnp.bfloat16)
    piece_spec = pl.BlockSpec((1, NZH, rows, width), lambda i: (i, 0, 0, 0))
    return pl.pallas_call(
        project_kernel,
        out_shape=(piece, piece),
        grid=(NY,),
        in_specs=[
            pl.BlockSpec(memory_space=pltpu.SMEM),
            pl.BlockSpec(parts.shape, lambda i: (0, 0, 0)),
            pl.BlockSpec((weight.shape[0], step), lambda i: (0, i)),
        ],
        out_specs=(piece_spec, piece_spec),
        scratch_shapes=[pltpu.VMEM((rows, HEADS * VD), jnp.bfloat16)],
        compiler_params=pltpu.CompilerParams(vmem_limit_bytes=VMEM_LIMIT),
    )(where, parts, weight)


def shifted(value, axis, size, by):
    return lax.ppermute(value, axis, [(i, (i + by) % size) for i in range(size)])


def swapped(value, axis):
    return shifted(value, axis, 2, 1)


def key_places(spans, x, c):
    row = jnp.arange(NY * NZL * NZH * 8, dtype=jnp.int32)
    y = row // (NZL * NZH * 8)
    zl = row // (NZH * 8) % NZL
    zh = row // 8 % NZH
    span = (zl * NX + x) * 2 + y // 2
    table = jnp.arange(spans.shape[0], dtype=jnp.int32)
    picked = jnp.sum(jnp.where(span[:, None] == table[None, :], spans[None, :], 0), axis=1)
    return (picked * SPAN + (y % 2) * 32 + zh * 16 + c * 8 + row % 8)[None, :]


def on_device(query_plain, query_rotary, latent_keys, span_order, key_up, value_up, output_weight):
    x = lax.axis_index("x")
    c = lax.axis_index("c")
    where = jnp.stack([lax.axis_index(CTX), lax.axis_index(TP)]).astype(jnp.int32)
    sent_keys, queries = prepare(where, span_order, query_plain, query_rotary, latent_keys)
    blocks = [queries] + [shifted(queries, "x", NX, k) for k in (1, 2, 3)]
    along_z = lax.all_to_all(sent_keys, ("zl", "zh"), split_axis=0, concat_axis=0, tiled=True)
    along_z = along_z.reshape(1, NZL * NZH * 8, KEYW)
    along_y = lax.all_to_all(
        jnp.broadcast_to(along_z, (NY, *along_z.shape[1:])), "y", split_axis=0, concat_axis=0, tiled=True
    )
    own = along_y.reshape(NY * NZL * NZH * 8, KEYW)
    other = swapped(own, "c")
    places = (key_places(span_order, x, c), key_places(span_order, x, 1 - c))
    parts = attend(where, span_order, blocks, own, other, places, key_up, value_up)
    parts = lax.all_to_all(parts, "x", split_axis=0, concat_axis=0, tiled=True)
    send, keep = project(where, parts, output_weight)
    both = (keep.astype(jnp.float32) + swapped(send, "c").astype(jnp.float32)).astype(jnp.bfloat16)
    over_y = lax.all_to_all(both, "y", split_axis=0, concat_axis=0, tiled=True)
    summed = jnp.sum(over_y.astype(jnp.float32), axis=0)
    zh = lax.axis_index("zh")
    mine = jnp.where(zh == 0, summed[0], summed[1])
    theirs = jnp.where(zh == 0, summed[1], summed[0]).astype(jnp.bfloat16)
    return (mine + swapped(theirs, "zh").astype(jnp.float32)).astype(jnp.bfloat16)


def solution(mesh):
    finer = Mesh(
        mesh.devices.reshape(NZL, NX, NY, NZH, NC), ("zl", "x", "y", "zh", "c")
    )
    in_specs = (
        P(CTX, TP),
        P(CTX, TP),
        P(CTX + TP, None),
        P(),
        P(TP, None, None),
        P(TP, None, None),
        P(TP, None),
    )
    return jax.shard_map(
        on_device, mesh=finer, in_specs=in_specs, out_specs=P(CTX, TP), check_vma=False
    )
```

```python
import functools
import math

import jax
import jax.numpy as jnp
import numpy as np
from jax import lax
from jax.experimental import pallas as pl
from jax.experimental.pallas import tpu as pltpu
from jax.sharding import Mesh
from jax.sharding import PartitionSpec as P

NZL, NX, NY, NZH, NC = 8, 4, 4, 2, 2
CTX = ("zl", "x")
TP = ("y", "zh", "c")

SPAN = 64
ROPE = 64
LAT = 512
NOPE = 128
VD = 128
HEADS = 4
KEYW = LAT + ROPE
ROWW = 640
GROUP = NZL * NZH
NSPAN = 2 * NZL
CHUNK = 256
QW = HEADS * (NOPE + ROPE)
OUTW = HEADS * VD + 128
BASE = 10000.0
LOW = -1e30
VMEM_LIMIT = 48 * 1024 * 1024


def rotary_tables():
    lane = np.arange(128)
    freq = BASE ** (-2.0 * (lane % 32) / ROPE)
    sign = np.where(lane % 64 < 32, -1.0, 1.0)
    start = (np.arange(64) * SPAN)[:, None] * freq[None, :]
    offset = np.arange(SPAN)[:, None] * freq[None, :]
    tables = [np.cos(start), sign * np.sin(start), np.cos(offset), sign * np.sin(offset)]
    return np.stack(tables).astype(np.float32)


def turn(values, cosine, signed_sine):
    lane = lax.broadcasted_iota(jnp.int32, values.shape, 1)
    partner = jnp.where(
        lane % 64 < 32, pltpu.roll(values, 96, axis=1), pltpu.roll(values, 32, axis=1)
    )
    return values * cosine + partner * signed_sine


def angle_of(tables_ref, span, offset_rows):
    cos_a = tables_ref[0, pl.ds(span, 1), :]
    sin_a = tables_ref[1, pl.ds(span, 1), :]
    cos_b = tables_ref[2, offset_rows, :]
    sin_b = tables_ref[3, offset_rows, :]
    return cos_a * cos_b - sin_a * sin_b, sin_a * cos_b + cos_a * sin_b


def own_ctx():
    return lax.axis_index("zl") * NX + lax.axis_index("x")


def own_tp():
    return (lax.axis_index("y") * NZH + lax.axis_index("zh")) * NC + lax.axis_index("c")


def keys_kernel(spans_ref, keys_ref, tables_ref, out_ref):
    tp = own_tp()
    span = spans_ref[own_ctx() * 2 + tp // 8]
    first = pl.multiple_of((tp % 8) * 8, 8)
    cosine, sine = angle_of(tables_ref, span, pl.ds(first, 8))
    tail = keys_ref[:, LAT:].astype(jnp.float32)
    turned = turn(jnp.concatenate([tail, tail], axis=1), cosine, sine).astype(jnp.bfloat16)
    for k in range(GROUP):
        out_ref[k, :, :LAT] = keys_ref[:, :LAT]
        out_ref[k, :, LAT:] = turned


def queries_kernel(spans_ref, plain_ref, rotary_ref, tables_ref, after_ref, out_ref):
    out_ref[:, : HEADS * NOPE] = plain_ref[...]
    for s in range(2):
        rows = slice(s * SPAN, (s + 1) * SPAN)
        cosine, sine = angle_of(tables_ref, spans_ref[own_ctx() * 2 + s], pl.ds(0, SPAN))
        for j in range(HEADS * ROPE // 128):
            part = rotary_ref[rows, j * 128 : (j + 1) * 128].astype(jnp.float32)
            at = HEADS * NOPE + j * 128
            out_ref[rows, at : at + 128] = turn(part, cosine, sine).astype(jnp.bfloat16)


SMEM = pl.BlockSpec(memory_space=pltpu.SMEM)
WHOLE = pl.BlockSpec(memory_space=pltpu.VMEM)


def attend_kernel(spans_ref, q0, q1, q2, q3, own_ref, other_ref, up_ref, value_ref, out_ref, query, sorted_keys, contexts):
    zl = lax.axis_index("zl")
    x = lax.axis_index("x")
    c = lax.axis_index("c")
    scale = math.log2(math.e) / math.sqrt(NOPE + ROPE)

    places = [spans_ref[((i // 2) * NX + x) * 2 + i % 2] for i in range(NSPAN)]

    def earlier(place):
        return functools.reduce(jnp.add, [(p < place).astype(jnp.int32) for p in places])

    for i in range(NSPAN):
        rank = earlier(places[i])
        for half, keys in enumerate((own_ref, other_ref)):
            for low in range(2):
                source = ((i % 2) * 2 + low) * GROUP * 8 + (i // 2) * NZH * 8
                target = pl.multiple_of(rank * SPAN + half * 32 + low * 16, 16)
                sorted_keys[pl.ds(target, 16), :] = keys[source : source + 16, :]

    blocks = (q0, q1, q2, q3)
    for h in range(HEADS):
        plain = jnp.concatenate([block[:, h * NOPE : (h + 1) * NOPE] for block in blocks], axis=0)
        absorbed = jnp.dot(plain, up_ref[h], preferred_element_type=jnp.float32).astype(jnp.bfloat16)
        first = HEADS * NOPE + h * ROPE
        at = slice(h * SPAN, (h + 1) * SPAN)
        for b in range(2 * NX):
            query[b, at, :LAT] = absorbed[b * SPAN : (b + 1) * SPAN]
            query[b, at, LAT:] = blocks[b // 2][(b % 2) * SPAN : (b % 2 + 1) * SPAN, first : first + ROPE]

    column = lax.broadcasted_iota(jnp.int32, (1, CHUNK), 1)
    core = jnp.where(column // 32 % 2 == 0, c, 1 - c)
    key_order = column // SPAN * SPAN + column // 16 % 2 * 32 + column // 8 % 2 * 16 + core * 8 + column % 8
    token = lax.broadcasted_iota(jnp.int32, (HEADS * SPAN, 1), 0) % SPAN
    lane = lax.broadcasted_iota(jnp.int32, (SPAN, 128), 1)
    dims = (((1,), (1,)), ((), ()))

    def one_span(b, carry):
        block = (x + NX - b // 2) % NX
        first_row = pl.multiple_of((b % 2) * SPAN, SPAN)
        below = earlier(spans_ref[(zl * NX + block) * 2 + b % 2])
        diagonal = block == x
        chunks = (below + diagonal.astype(jnp.int32) + CHUNK // SPAN - 1) // (CHUNK // SPAN)
        limit = below * SPAN + jnp.where(diagonal, token, -1)

        @pl.when(chunks == 0)
        def _():
            for h in range(HEADS):
                contexts[h, pl.ds(pl.multiple_of(b * SPAN, SPAN), SPAN), :] = jnp.zeros((SPAN, LAT), jnp.bfloat16)
            out_ref[block, pl.ds(first_row, SPAN), HEADS * VD :] = jnp.where(
                lane < HEADS, LOW, 0.0
            ).astype(jnp.bfloat16)

        for count in range(1, NSPAN * SPAN // CHUNK + 1):

            @pl.when(chunks == count)
            def _(count=count):
                rows = query[b]
                scores = []
                for n in range(count):
                    raw = lax.dot_general(
                        rows,
                        sorted_keys[n * CHUNK : (n + 1) * CHUNK, :KEYW],
                        dims,
                        preferred_element_type=jnp.float32,
                    ) * scale
                    if n == count - 1:
                        raw = jnp.where(key_order + n * CHUNK <= limit, raw, LOW)
                    scores.append(raw)
                highest = functools.reduce(jnp.maximum, [jnp.max(v, axis=1, keepdims=True) for v in scores])
                total = None
                context = None
                for n in range(count):
                    raised = jnp.exp2(scores[n] - highest)
                    part_sum = jnp.sum(raised, axis=1, keepdims=True)
                    part = jnp.dot(
                        raised.astype(jnp.bfloat16),
                        sorted_keys[n * CHUNK : (n + 1) * CHUNK, :LAT],
                        preferred_element_type=jnp.float32,
                    )
                    total = part_sum if total is None else total + part_sum
                    context = part if context is None else context + part
                context = (context * (1.0 / total)).astype(jnp.bfloat16)
                log_sum = highest + jnp.log2(total)
                high = log_sum.astype(jnp.bfloat16).astype(jnp.float32)
                rest = log_sum - high
                middle = rest.astype(jnp.bfloat16).astype(jnp.float32)
                packed = jnp.zeros((SPAN, 128), jnp.float32)
                for h in range(HEADS):
                    at = slice(h * SPAN, (h + 1) * SPAN)
                    contexts[h, pl.ds(pl.multiple_of(b * SPAN, SPAN), SPAN), :] = context[at]
                    for n, part in enumerate((high, middle, rest - middle)):
                        packed = jnp.where(lane == n * HEADS + h, part[at], packed)
                out_ref[block, pl.ds(first_row, SPAN), HEADS * VD :] = packed.astype(jnp.bfloat16)

        return carry

    lax.fori_loop(0, 2 * NX, one_span, 0)

    for h in range(HEADS):
        values = jnp.dot(contexts[h], value_ref[h], preferred_element_type=jnp.float32).astype(jnp.bfloat16)
        for k in range(NX):
            out_ref[(x + NX - k) % NX, :, h * VD : (h + 1) * VD] = values[k * 2 * SPAN : (k + 1) * 2 * SPAN]


def attend(spans, blocks, own, other, key_up, value_up):
    return pl.pallas_call(
        attend_kernel,
        out_shape=jax.ShapeDtypeStruct((NX, 2 * SPAN, OUTW), jnp.bfloat16),
        in_specs=[SMEM] + [WHOLE] * 8,
        out_specs=WHOLE,
        scratch_shapes=[
            pltpu.VMEM((2 * NX, HEADS * SPAN, KEYW), jnp.bfloat16),
            pltpu.VMEM((NSPAN * SPAN, ROWW), jnp.bfloat16),
            pltpu.VMEM((HEADS, NX * 2 * SPAN, LAT), jnp.bfloat16),
        ],
        compiler_params=pltpu.CompilerParams(vmem_limit_bytes=VMEM_LIMIT),
    )(spans, *blocks, own, other, key_up, value_up)


def project_kernel(parts_ref, weight_ref, send_ref, keep_ref):
    c = lax.axis_index("c")
    packed = [parts_ref[i, :, HEADS * VD :].astype(jnp.float32) for i in range(NX)]
    heads = []
    for h in range(HEADS):
        logs = [
            (p[:, h : h + 1] + p[:, HEADS + h : HEADS + h + 1]) + p[:, 2 * HEADS + h : 2 * HEADS + h + 1]
            for p in packed
        ]
        highest = functools.reduce(jnp.maximum, logs)
        shares = [jnp.exp2(v - highest) for v in logs]
        inverse = 1.0 / functools.reduce(jnp.add, shares)
        merged = functools.reduce(
            jnp.add,
            [
                (shares[i] * inverse) * parts_ref[i, :, h * VD : (h + 1) * VD].astype(jnp.float32)
                for i in range(NX)
            ],
        )
        heads.append(merged.astype(jnp.bfloat16))
    head_out = jnp.concatenate(heads, axis=1)
    step = weight_ref.shape[1] // NY
    width = step // (NZH * NC)
    for y in range(NY):
        result = jnp.dot(
            head_out, weight_ref[:, y * step : (y + 1) * step], preferred_element_type=jnp.float32
        ).T.astype(jnp.bfloat16)
        for zh in range(NZH):
            even = result[2 * zh * width : (2 * zh + 1) * width]
            odd = result[(2 * zh + 1) * width : (2 * zh + 2) * width]
            keep_ref[y, zh] = jnp.where(c == 0, even, odd)
            send_ref[y, zh] = jnp.where(c == 0, odd, even)


def project(parts, weight):
    rows = parts.shape[1]
    width = weight.shape[1] // (NY * NZH * NC)
    piece = jax.ShapeDtypeStruct((NY, NZH, width, rows), jnp.bfloat16)
    return pl.pallas_call(
        project_kernel,
        out_shape=(piece, piece),
        in_specs=[WHOLE, WHOLE],
        out_specs=(WHOLE, WHOLE),
        compiler_params=pltpu.CompilerParams(vmem_limit_bytes=VMEM_LIMIT),
    )(parts, weight)


def swapped(value, axis):
    return lax.ppermute(value, axis, [(0, 1), (1, 0)])


def exchanged(value, axis):
    return lax.all_to_all(value, axis, split_axis=0, concat_axis=0, tiled=True)


def on_device(query_plain, query_rotary, latent_keys, span_order, key_up, value_up, output_weight):
    zh = lax.axis_index("zh")
    tables = jnp.asarray(rotary_tables())
    sent_keys = pl.pallas_call(
        keys_kernel,
        out_shape=jax.ShapeDtypeStruct((GROUP, 8, ROWW), jnp.bfloat16),
        in_specs=[SMEM, WHOLE, WHOLE],
        out_specs=WHOLE,
    )(span_order, latent_keys, tables)
    queries = pl.pallas_call(
        queries_kernel,
        out_shape=jax.ShapeDtypeStruct((2 * SPAN, QW), jnp.bfloat16),
        in_specs=[SMEM, WHOLE, WHOLE, WHOLE, pl.BlockSpec(memory_space=pl.ANY)],
        out_specs=WHOLE,
    )(span_order, query_plain, query_rotary, tables, sent_keys)
    along_z = exchanged(sent_keys, ("zl", "zh")).reshape(GROUP * 8, ROWW)
    blocks = [queries] + [
        lax.ppermute(queries, "x", [(i, (i + k) % NX) for i in range(NX)]) for k in range(1, NX)
    ]
    along_z, *blocks = lax.optimization_barrier((along_z, *blocks))
    own = exchanged(jnp.broadcast_to(along_z[None], (NY, GROUP * 8, ROWW)), "y").reshape(NY * GROUP * 8, ROWW)
    other = swapped(own, "c")
    parts = attend(span_order, blocks, own, other, key_up, value_up)
    send, keep = project(exchanged(parts, "x"), output_weight)
    both = (keep.astype(jnp.float32) + swapped(send, "c").astype(jnp.float32)).astype(jnp.bfloat16)
    over_y = exchanged(both, "y").astype(jnp.float32)
    mine = jnp.sum(lax.dynamic_index_in_dim(over_y, zh, 1, keepdims=False), axis=0)
    theirs = jnp.sum(lax.dynamic_index_in_dim(over_y, 1 - zh, 1, keepdims=False), axis=0).astype(jnp.bfloat16)
    return (mine + swapped(theirs, "zh").astype(jnp.float32)).astype(jnp.bfloat16).T


def solution(mesh):
    finer = Mesh(
        mesh.devices.reshape(NZL, NX, NY, NZH, NC), ("zl", "x", "y", "zh", "c")
    )
    in_specs = (
        P(CTX, TP),
        P(CTX, TP),
        P(CTX + TP, None),
        P(),
        P(TP, None, None),
        P(TP, None, None),
        P(TP, None),
    )
    return jax.shard_map(
        on_device, mesh=finer, in_specs=in_specs, out_specs=P(CTX, TP), check_vma=False
    )
```

```python
import functools
import math

import jax
import jax.numpy as jnp
import numpy as np
from jax import lax
from jax.experimental import pallas as pl
from jax.experimental.pallas import tpu as pltpu
from jax.sharding import Mesh
from jax.sharding import PartitionSpec as P

NZL, NX, NY, NZH, NC = 8, 4, 4, 2, 2
CTX = ("zl", "x")
TP = ("y", "zh", "c")

SPAN = 64
ROPE = 64
LAT = 512
NOPE = 128
VD = 128
HEADS = 4
KEYW = LAT + ROPE
ROWW = 640
GROUP = NZL * NZH
NSPAN = 2 * NZL
CHUNK = 256
GROUPED = 4
QW = HEADS * (NOPE + ROPE)
PARTROWS = HEADS * (VD + 16)
BASE = 10000.0
LOW = -1e30
SCALE = math.log2(math.e) / math.sqrt(NOPE + ROPE)
VMEM_LIMIT = 48 * 1024 * 1024


def rotary_tables():
    lane = np.arange(128)
    freq = BASE ** (-2.0 * (lane % 32) / ROPE)
    sign = np.where(lane % 64 < 32, -1.0, 1.0)
    start = (np.arange(64) * SPAN)[:, None] * freq[None, :]
    offset = np.arange(SPAN)[:, None] * freq[None, :]
    tables = [np.cos(start), sign * np.sin(start), np.cos(offset), sign * np.sin(offset)]
    return np.stack(tables).astype(np.float32)


def turn(values, cosine, signed_sine):
    lane = lax.broadcasted_iota(jnp.int32, values.shape, 1)
    partner = jnp.where(
        lane % 64 < 32, pltpu.roll(values, 96, axis=1), pltpu.roll(values, 32, axis=1)
    )
    return values * cosine + partner * signed_sine


def angle_of(tables_ref, span, offset_rows):
    cos_a = tables_ref[0, pl.ds(span, 1), :]
    sin_a = tables_ref[1, pl.ds(span, 1), :]
    cos_b = tables_ref[2, offset_rows, :]
    sin_b = tables_ref[3, offset_rows, :]
    return cos_a * cos_b - sin_a * sin_b, sin_a * cos_b + cos_a * sin_b


def own_ctx():
    return lax.axis_index("zl") * NX + lax.axis_index("x")


def own_tp():
    return (lax.axis_index("y") * NZH + lax.axis_index("zh")) * NC + lax.axis_index("c")


def keys_kernel(spans_ref, keys_ref, tables_ref, out_ref):
    tp = own_tp()
    span = spans_ref[own_ctx() * 2 + tp // 8]
    first = pl.multiple_of((tp % 8) * 8, 8)
    cosine, sine = angle_of(tables_ref, span, pl.ds(first, 8))
    tail = keys_ref[:, LAT:].astype(jnp.float32)
    turned = turn(jnp.concatenate([tail, tail], axis=1), cosine, sine).astype(jnp.bfloat16)
    for k in range(GROUP):
        out_ref[k, :, :LAT] = keys_ref[:, :LAT]
        out_ref[k, :, LAT:] = turned


def queries_kernel(spans_ref, plain_ref, rotary_ref, tables_ref, after_ref, out_ref, kept_spans_ref):
    out_ref[:, : HEADS * NOPE] = plain_ref[...]
    for s in range(2):
        rows = slice(s * SPAN, (s + 1) * SPAN)
        cosine, sine = angle_of(tables_ref, spans_ref[own_ctx() * 2 + s], pl.ds(0, SPAN))
        for j in range(HEADS * ROPE // 128):
            part = rotary_ref[rows, j * 128 : (j + 1) * 128].astype(jnp.float32)
            at = HEADS * NOPE + j * 128
            out_ref[rows, at : at + 128] = (turn(part, cosine, sine) * SCALE).astype(jnp.bfloat16)
    for i in range(kept_spans_ref.shape[0]):
        kept_spans_ref[i] = spans_ref[i]


SMEM = pl.BlockSpec(memory_space=pltpu.SMEM)
WHOLE = pl.BlockSpec(memory_space=pltpu.VMEM)


def absorb_kernel(q0, q1, q2, q3, up_ref, value_ref, query, turned_value):
    blocks = (q0, q1, q2, q3)
    for h in range(HEADS):
        plain = jnp.concatenate([block[:, h * NOPE : (h + 1) * NOPE] for block in blocks], axis=0)
        absorbed = (jnp.dot(plain, up_ref[h], preferred_element_type=jnp.float32) * SCALE).astype(jnp.bfloat16)
        first = HEADS * NOPE + h * ROPE
        at = slice(h * SPAN, (h + 1) * SPAN)
        for b in range(2 * NX):
            query[b, at, :LAT] = absorbed[b * SPAN : (b + 1) * SPAN]
            query[b, at, LAT:] = blocks[b // 2][(b % 2) * SPAN : (b % 2 + 1) * SPAN, first : first + ROPE]
    for h in range(HEADS):
        turned_value[h] = value_ref[h].T


def absorb(blocks, key_up, value_up):
    return pl.pallas_call(
        absorb_kernel,
        out_shape=(
            jax.ShapeDtypeStruct((2 * NX, HEADS * SPAN, KEYW), jnp.bfloat16),
            jax.ShapeDtypeStruct((HEADS, VD, LAT), jnp.bfloat16),
        ),
        in_specs=[WHOLE] * 6,
        out_specs=(WHOLE, WHOLE),
        compiler_params=pltpu.CompilerParams(vmem_limit_bytes=VMEM_LIMIT),
    )(*blocks, key_up, value_up)


def attend_kernel(
    spans_ref, query, own_ref, other_ref, value_ref, out_ref, sorted_keys, latent, contexts, order
):
    zl = lax.axis_index("zl")
    x = lax.axis_index("x")
    c = lax.axis_index("c")

    places = [spans_ref[((i // 2) * NX + x) * 2 + i % 2] for i in range(NSPAN)]

    def earlier(place, among):
        return functools.reduce(jnp.add, [(p < place).astype(jnp.int32) for p in among])

    for i in range(NSPAN):
        rank = earlier(places[i], places)
        for half, keys in enumerate((own_ref, other_ref)):
            for low in range(2):
                source = ((i % 2) * 2 + low) * GROUP * 8 + (i // 2) * NZH * 8
                target = pl.multiple_of(rank * SPAN + half * 32 + low * 16, 16)
                sorted_keys[pl.ds(target, 16), :] = keys[source : source + 16, :]

    asking = [spans_ref[(zl * NX + (x + NX - b // 2) % NX) * 2 + b % 2] for b in range(2 * NX)]
    for b in range(2 * NX):
        order[earlier(asking[b], asking)] = b

    for n in range(NSPAN * SPAN // CHUNK):
        at = slice(n * CHUNK, (n + 1) * CHUNK)
        latent[:, at] = sorted_keys[at, :LAT].T

    row = lax.broadcasted_iota(jnp.int32, (CHUNK, HEADS * SPAN), 0)
    core = jnp.where(row // 32 % 2 == 0, c, 1 - c)
    key_order = row // SPAN * SPAN + row // 16 % 2 * 32 + row // 8 % 2 * 16 + core * 8 + row % 8
    token = lax.broadcasted_iota(jnp.int32, (1, HEADS * SPAN), 1) % SPAN
    dims = (((1,), (1,)), ((), ()))

    def some_spans(turn_of, carry):
        spans = [order[GROUPED * turn_of + i] for i in range(GROUPED)]
        limits = []
        for b in spans:
            source = (x + NX - b // 2) % NX
            below = earlier(spans_ref[(zl * NX + source) * 2 + b % 2], places)
            limits.append(below * SPAN + jnp.where(source == x, token, -1))
            needed = below + (source == x).astype(jnp.int32)
        chunks = jnp.maximum((needed + CHUNK // SPAN - 1) // (CHUNK // SPAN), 1)

        for count in range(1, NSPAN * SPAN // CHUNK + 1):

            @pl.when(chunks == count)
            def _(count=count):
                products = [
                    [
                        lax.dot_general(
                            sorted_keys[n * CHUNK : (n + 1) * CHUNK, :KEYW],
                            query[b],
                            dims,
                            preferred_element_type=jnp.float32,
                        )
                        for n in range(count)
                    ]
                    for b in spans
                ]
                for b, limit, scores in zip(spans, limits, products):
                    scores = [
                        jnp.where(key_order <= limit - n * CHUNK, score, LOW) for n, score in enumerate(scores)
                    ]
                    highest = functools.reduce(jnp.maximum, [jnp.max(v, axis=0, keepdims=True) for v in scores])
                    raised = [jnp.exp2(score - highest) for score in scores]
                    total = functools.reduce(jnp.add, [jnp.sum(v, axis=0, keepdims=True) for v in raised])
                    context = jnp.dot(
                        latent[:, : count * CHUNK],
                        jnp.concatenate([v.astype(jnp.bfloat16) for v in raised], axis=0),
                        preferred_element_type=jnp.float32,
                    )
                    contexts[b, :LAT, :] = (context * (1.0 / total)).astype(jnp.bfloat16)
                    log_sum = highest + jnp.log2(total)
                    high = log_sum.astype(jnp.bfloat16).astype(jnp.float32)
                    rest = log_sum - high
                    middle = rest.astype(jnp.bfloat16).astype(jnp.float32)
                    place = lax.broadcasted_iota(jnp.int32, (16, HEADS * SPAN), 0)
                    packed = jnp.where(place == 0, high, jnp.where(place == 1, middle, rest - middle))
                    contexts[b, LAT:, :] = packed.astype(jnp.bfloat16)

        return carry

    lax.fori_loop(0, 2 * NX // GROUPED, some_spans, 0)

    for h in range(HEADS):
        at = slice(h * SPAN, (h + 1) * SPAN)
        joined = jnp.concatenate([contexts[b, :LAT, at] for b in range(2 * NX)], axis=1)
        values = jnp.dot(value_ref[h], joined, preferred_element_type=jnp.float32).astype(jnp.bfloat16)
        logs = jnp.concatenate([contexts[b, LAT:, at] for b in range(2 * NX)], axis=1)
        for k in range(NX):
            tokens = slice(k * 2 * SPAN, (k + 1) * 2 * SPAN)
            out_ref[(x + NX - k) % NX, h * VD : (h + 1) * VD, :] = values[:, tokens]
            out_ref[(x + NX - k) % NX, HEADS * VD + h * 16 : HEADS * VD + (h + 1) * 16, :] = logs[:, tokens]


def attend(spans, query, own, other, turned_value):
    return pl.pallas_call(
        attend_kernel,
        out_shape=jax.ShapeDtypeStruct((NX, PARTROWS, 2 * SPAN), jnp.bfloat16),
        in_specs=[SMEM] + [WHOLE] * 4,
        out_specs=WHOLE,
        scratch_shapes=[
            pltpu.VMEM((NSPAN * SPAN, ROWW), jnp.bfloat16),
            pltpu.VMEM((LAT, NSPAN * SPAN), jnp.bfloat16),
            pltpu.VMEM((2 * NX, LAT + 16, HEADS * SPAN), jnp.bfloat16),
            pltpu.SMEM((2 * NX,), jnp.int32),
        ],
        compiler_params=pltpu.CompilerParams(vmem_limit_bytes=VMEM_LIMIT),
    )(spans, query, own, other, turned_value)


def project_kernel(parts_ref, weight_ref, send_ref, keep_ref):
    c = lax.axis_index("c")
    heads = []
    for h in range(HEADS):
        at = HEADS * VD + h * 16
        packed = [parts_ref[i, at : at + 16, :].astype(jnp.float32) for i in range(NX)]
        logs = [(p[0:1] + p[1:2]) + p[2:3] for p in packed]
        highest = functools.reduce(jnp.maximum, logs)
        shares = [jnp.exp2(v - highest) for v in logs]
        inverse = 1.0 / functools.reduce(jnp.add, shares)
        merged = functools.reduce(
            jnp.add,
            [
                (shares[i] * inverse) * parts_ref[i, h * VD : (h + 1) * VD, :].astype(jnp.float32)
                for i in range(NX)
            ],
        )
        heads.append(merged.T.astype(jnp.bfloat16))
    head_out = jnp.concatenate(heads, axis=1)
    step = weight_ref.shape[1] // NY
    width = step // (NZH * NC)
    for y in range(NY):
        result = jnp.dot(
            head_out, weight_ref[:, y * step : (y + 1) * step], preferred_element_type=jnp.float32
        ).T.astype(jnp.bfloat16)
        for zh in range(NZH):
            even = result[2 * zh * width : (2 * zh + 1) * width]
            odd = result[(2 * zh + 1) * width : (2 * zh + 2) * width]
            keep_ref[y, zh] = jnp.where(c == 0, even, odd)
            send_ref[y, zh] = jnp.where(c == 0, odd, even)


def project(parts, weight):
    width = weight.shape[1] // (NY * NZH * NC)
    piece = jax.ShapeDtypeStruct((NY, NZH, width, 2 * SPAN), jnp.bfloat16)
    return pl.pallas_call(
        project_kernel,
        out_shape=(piece, piece),
        in_specs=[WHOLE, WHOLE],
        out_specs=(WHOLE, WHOLE),
        compiler_params=pltpu.CompilerParams(vmem_limit_bytes=VMEM_LIMIT),
    )(parts, weight)


def swapped(value, axis):
    return lax.ppermute(value, axis, [(0, 1), (1, 0)])


def exchanged(value, axis):
    return lax.all_to_all(value, axis, split_axis=0, concat_axis=0, tiled=True)


def on_device(query_plain, query_rotary, latent_keys, span_order, key_up, value_up, output_weight):
    zh = lax.axis_index("zh")
    tables = jnp.asarray(rotary_tables())
    sent_keys = pl.pallas_call(
        keys_kernel,
        out_shape=jax.ShapeDtypeStruct((GROUP, 8, ROWW), jnp.bfloat16),
        in_specs=[SMEM, WHOLE, WHOLE],
        out_specs=WHOLE,
    )(span_order, latent_keys, tables)
    rows = jax.ShapeDtypeStruct((2 * SPAN, QW), jnp.bfloat16)
    queries, kept_spans = pl.pallas_call(
        queries_kernel,
        out_shape=(rows, jax.ShapeDtypeStruct(span_order.shape, span_order.dtype)),
        in_specs=[SMEM, WHOLE, WHOLE, WHOLE, pl.BlockSpec(memory_space=pl.ANY)],
        out_specs=(WHOLE, SMEM),
    )(span_order, query_plain, query_rotary, tables, sent_keys)
    along_z = exchanged(sent_keys, ("zl", "zh")).reshape(GROUP * 8, ROWW)
    blocks = [queries] + [
        lax.ppermute(queries, "x", [(i, (i + k) % NX) for i in range(NX)]) for k in range(1, NX)
    ]
    along_z, blocks[1] = lax.optimization_barrier((along_z, blocks[1]))
    own = exchanged(jnp.broadcast_to(along_z[None], (NY, GROUP * 8, ROWW)), "y").reshape(NY * GROUP * 8, ROWW)
    own, blocks[2], blocks[3] = lax.optimization_barrier((own, blocks[2], blocks[3]))
    other = swapped(own, "c")
    query, turned_value = absorb(blocks, key_up, value_up)
    parts = attend(kept_spans, query, own, other, turned_value)
    send, keep = project(exchanged(parts, "x"), output_weight)
    both = (keep.astype(jnp.float32) + swapped(send, "c").astype(jnp.float32)).astype(jnp.bfloat16)
    over_y = exchanged(both, "y").astype(jnp.float32)
    mine = jnp.sum(lax.dynamic_index_in_dim(over_y, zh, 1, keepdims=False), axis=0)
    theirs = jnp.sum(lax.dynamic_index_in_dim(over_y, 1 - zh, 1, keepdims=False), axis=0).astype(jnp.bfloat16)
    return (mine + swapped(theirs, "zh").astype(jnp.float32)).astype(jnp.bfloat16).T


def solution(mesh):
    finer = Mesh(
        mesh.devices.reshape(NZL, NX, NY, NZH, NC), ("zl", "x", "y", "zh", "c")
    )
    in_specs = (
        P(CTX, TP),
        P(CTX, TP),
        P(CTX + TP, None),
        P(),
        P(TP, None, None),
        P(TP, None, None),
        P(TP, None),
    )
    return jax.shard_map(
        on_device, mesh=finer, in_specs=in_specs, out_specs=P(CTX, TP), check_vma=False
    )
```

```python
import functools
import math

import jax
import jax.numpy as jnp
import numpy as np
from jax import lax
from jax.experimental import pallas as pl
from jax.experimental.pallas import tpu as pltpu
from jax.sharding import Mesh
from jax.sharding import PartitionSpec as P

NZL, NX, NY, NZH, NC = 8, 4, 4, 2, 2
CTX = ("zl", "x")
TP = ("y", "zh", "c")

SPAN = 64
ROPE = 64
LAT = 512
NOPE = 128
VD = 128
HEADS = 4
KEYW = LAT + ROPE
ROWW = 640
GROUP = NZL * NZH
NSPAN = 2 * NZL
CHUNK = 256
GROUPED = 4
QW = HEADS * (NOPE + ROPE)
PARTROWS = HEADS * VD + 16
BASE = 10000.0
LOW = -1e30
SCALE = math.log2(math.e) / math.sqrt(NOPE + ROPE)
VMEM_LIMIT = 48 * 1024 * 1024


def rotary_tables():
    lane = np.arange(128)
    freq = BASE ** (-2.0 * (lane % 32) / ROPE)
    sign = np.where(lane % 64 < 32, -1.0, 1.0)
    start = (np.arange(64) * SPAN)[:, None] * freq[None, :]
    offset = np.arange(SPAN)[:, None] * freq[None, :]
    tables = [np.cos(start), sign * np.sin(start), np.cos(offset), sign * np.sin(offset)]
    return np.stack(tables).astype(np.float32)


def turn(values, cosine, signed_sine):
    lane = lax.broadcasted_iota(jnp.int32, values.shape, 1)
    partner = jnp.where(
        lane % 64 < 32, pltpu.roll(values, 96, axis=1), pltpu.roll(values, 32, axis=1)
    )
    return values * cosine + partner * signed_sine


def angle_of(tables_ref, span, offset_rows):
    cos_a = tables_ref[0, pl.ds(span, 1), :]
    sin_a = tables_ref[1, pl.ds(span, 1), :]
    cos_b = tables_ref[2, offset_rows, :]
    sin_b = tables_ref[3, offset_rows, :]
    return cos_a * cos_b - sin_a * sin_b, sin_a * cos_b + cos_a * sin_b


def own_ctx():
    return lax.axis_index("zl") * NX + lax.axis_index("x")


def own_tp():
    return (lax.axis_index("y") * NZH + lax.axis_index("zh")) * NC + lax.axis_index("c")


def keys_kernel(spans_ref, keys_ref, tables_ref, out_ref):
    tp = own_tp()
    span = spans_ref[own_ctx() * 2 + tp // 8]
    first = pl.multiple_of((tp % 8) * 8, 8)
    cosine, sine = angle_of(tables_ref, span, pl.ds(first, 8))
    tail = keys_ref[:, LAT:].astype(jnp.float32)
    turned = turn(jnp.concatenate([tail, tail], axis=1), cosine, sine).astype(jnp.bfloat16)
    for k in range(GROUP):
        out_ref[k, :, :LAT] = keys_ref[:, :LAT]
        out_ref[k, :, LAT:] = turned


def queries_kernel(spans_ref, plain_ref, rotary_ref, tables_ref, after_ref, out_ref, kept_spans_ref):
    out_ref[:, : HEADS * NOPE] = plain_ref[...]
    for s in range(2):
        rows = slice(s * SPAN, (s + 1) * SPAN)
        cosine, sine = angle_of(tables_ref, spans_ref[own_ctx() * 2 + s], pl.ds(0, SPAN))
        for j in range(HEADS * ROPE // 128):
            part = rotary_ref[rows, j * 128 : (j + 1) * 128].astype(jnp.float32)
            at = HEADS * NOPE + j * 128
            out_ref[rows, at : at + 128] = (turn(part, cosine, sine) * SCALE).astype(jnp.bfloat16)
    for i in range(kept_spans_ref.shape[0]):
        kept_spans_ref[i] = spans_ref[i]


SMEM = pl.BlockSpec(memory_space=pltpu.SMEM)
WHOLE = pl.BlockSpec(memory_space=pltpu.VMEM)
HBM = pl.BlockSpec(memory_space=pltpu.HBM)


def absorb_kernel(q0_hbm, q1, q2, q3, up_hbm, value_hbm, query, turned_value, q0, up_ref, value_ref, arrived):
    fetches = [
        pltpu.make_async_copy(source, target, arrived.at[i])
        for i, (source, target) in enumerate(((q0_hbm, q0), (up_hbm, up_ref), (value_hbm, value_ref)))
    ]
    for fetch in fetches:
        fetch.start()
    for fetch in fetches:
        fetch.wait()
    blocks = (q0, q1, q2, q3)
    for h in range(HEADS):
        plain = jnp.concatenate([block[:, h * NOPE : (h + 1) * NOPE] for block in blocks], axis=0)
        absorbed = (jnp.dot(plain, up_ref[h], preferred_element_type=jnp.float32) * SCALE).astype(jnp.bfloat16)
        first = HEADS * NOPE + h * ROPE
        at = slice(h * SPAN, (h + 1) * SPAN)
        for b in range(2 * NX):
            query[b, at, :LAT] = absorbed[b * SPAN : (b + 1) * SPAN]
            query[b, at, LAT:] = blocks[b // 2][(b % 2) * SPAN : (b % 2 + 1) * SPAN, first : first + ROPE]
    for h in range(HEADS):
        turned_value[h] = value_ref[h].T


def in_hbm(value):
    return pltpu.with_memory_space_constraint(value, pltpu.HBM)


def absorb(blocks, key_up, value_up):
    return pl.pallas_call(
        absorb_kernel,
        out_shape=(
            jax.ShapeDtypeStruct((2 * NX, HEADS * SPAN, KEYW), jnp.bfloat16),
            jax.ShapeDtypeStruct((HEADS, VD, LAT), jnp.bfloat16),
        ),
        in_specs=[HBM] + [WHOLE] * 3 + [HBM] * 2,
        out_specs=(WHOLE, WHOLE),
        scratch_shapes=[
            pltpu.VMEM(blocks[0].shape, jnp.bfloat16),
            pltpu.VMEM(key_up.shape, jnp.bfloat16),
            pltpu.VMEM(value_up.shape, jnp.bfloat16),
            pltpu.SemaphoreType.DMA((3,)),
        ],
        compiler_params=pltpu.CompilerParams(vmem_limit_bytes=VMEM_LIMIT),
    )(in_hbm(blocks[0]), *blocks[1:], in_hbm(key_up), in_hbm(value_up))


def attend_kernel(
    spans_ref, query, own_ref, other_ref, value_ref, out_ref, sorted_keys, latent, contexts, order
):
    zl = lax.axis_index("zl")
    x = lax.axis_index("x")
    c = lax.axis_index("c")

    places = [spans_ref[((i // 2) * NX + x) * 2 + i % 2] for i in range(NSPAN)]

    def earlier(place, among):
        return functools.reduce(jnp.add, [(p < place).astype(jnp.int32) for p in among])

    for i in range(NSPAN):
        rank = earlier(places[i], places)
        for half, keys in enumerate((own_ref, other_ref)):
            for low in range(2):
                source = ((i % 2) * 2 + low) * GROUP * 8 + (i // 2) * NZH * 8
                target = pl.multiple_of(rank * SPAN + half * 32 + low * 16, 16)
                sorted_keys[pl.ds(target, 16), :] = keys[source : source + 16, :]

    asking = [spans_ref[(zl * NX + (x + NX - b // 2) % NX) * 2 + b % 2] for b in range(2 * NX)]
    for b in range(2 * NX):
        order[earlier(asking[b], asking)] = b

    for n in range(NSPAN * SPAN // CHUNK):
        at = slice(n * CHUNK, (n + 1) * CHUNK)
        latent[:, at] = sorted_keys[at, :LAT].T

    row = lax.broadcasted_iota(jnp.int32, (CHUNK, HEADS * SPAN), 0)
    core = jnp.where(row // 32 % 2 == 0, c, 1 - c)
    key_order = row // SPAN * SPAN + row // 16 % 2 * 32 + row // 8 % 2 * 16 + core * 8 + row % 8
    token = lax.broadcasted_iota(jnp.int32, (1, HEADS * SPAN), 1) % SPAN
    head = lax.broadcasted_iota(jnp.int32, (16, HEADS * SPAN), 1) // SPAN
    dims = (((1,), (1,)), ((), ()))

    def some_spans(turn_of, carry):
        spans = [order[GROUPED * turn_of + i] for i in range(GROUPED)]
        limits = []
        for b in spans:
            source = (x + NX - b // 2) % NX
            below = earlier(spans_ref[(zl * NX + source) * 2 + b % 2], places)
            limits.append(below * SPAN + jnp.where(source == x, token, -1))
            needed = below + (source == x).astype(jnp.int32)
        chunks = jnp.maximum((needed + CHUNK // SPAN - 1) // (CHUNK // SPAN), 1)

        for count in range(1, NSPAN * SPAN // CHUNK + 1):

            @pl.when(chunks == count)
            def _(count=count):
                products = [
                    [
                        lax.dot_general(
                            sorted_keys[n * CHUNK : (n + 1) * CHUNK, :KEYW],
                            query[b],
                            dims,
                            preferred_element_type=jnp.float32,
                        )
                        for n in range(count)
                    ]
                    for b in spans
                ]
                for b, limit, scores in zip(spans, limits, products):
                    scores = [
                        jnp.where(key_order <= limit - n * CHUNK, score, LOW) for n, score in enumerate(scores)
                    ]
                    highest = functools.reduce(jnp.maximum, [jnp.max(v, axis=0, keepdims=True) for v in scores])
                    raised = [jnp.exp2(score - highest) for score in scores]
                    total = functools.reduce(jnp.add, [jnp.sum(v, axis=0, keepdims=True) for v in raised])
                    context = jnp.dot(
                        latent[:, : count * CHUNK],
                        jnp.concatenate([v.astype(jnp.bfloat16) for v in raised], axis=0),
                        preferred_element_type=jnp.float32,
                    )
                    contexts[b, :LAT, :] = (context * (1.0 / total)).astype(jnp.bfloat16)
                    log_sum = highest + jnp.log2(total)
                    high = log_sum.astype(jnp.bfloat16).astype(jnp.float32)
                    rest = log_sum - high
                    middle = rest.astype(jnp.bfloat16).astype(jnp.float32)
                    place = lax.broadcasted_iota(jnp.int32, (16, HEADS * SPAN), 0)
                    packed = jnp.where(place < HEADS, high, jnp.where(place < 2 * HEADS, middle, rest - middle))
                    packed = jnp.where((place < 3 * HEADS) & (place % HEADS == head), packed, 0.0)
                    contexts[b, LAT:, :] = packed.astype(jnp.bfloat16)

        return carry

    lax.fori_loop(0, 2 * NX // GROUPED, some_spans, 0)

    for h in range(HEADS):
        at = slice(h * SPAN, (h + 1) * SPAN)
        joined = jnp.concatenate([contexts[b, :LAT, at] for b in range(2 * NX)], axis=1)
        values = jnp.dot(value_ref[h], joined, preferred_element_type=jnp.float32).astype(jnp.bfloat16)
        for k in range(NX):
            tokens = slice(k * 2 * SPAN, (k + 1) * 2 * SPAN)
            out_ref[(x + NX - k) % NX, h * VD : (h + 1) * VD, :] = values[:, tokens]
    for k in range(NX):
        logs = [
            functools.reduce(
                jnp.add,
                [
                    contexts[b, LAT:, h * SPAN : (h + 1) * SPAN].astype(jnp.float32)
                    for h in range(HEADS)
                ],
            )
            for b in (2 * k, 2 * k + 1)
        ]
        out_ref[(x + NX - k) % NX, HEADS * VD :, :] = jnp.concatenate(logs, axis=1).astype(jnp.bfloat16)


def attend(spans, query, own, other, turned_value):
    return pl.pallas_call(
        attend_kernel,
        out_shape=jax.ShapeDtypeStruct((NX, PARTROWS, 2 * SPAN), jnp.bfloat16),
        in_specs=[SMEM] + [WHOLE] * 4,
        out_specs=WHOLE,
        scratch_shapes=[
            pltpu.VMEM((NSPAN * SPAN, ROWW), jnp.bfloat16),
            pltpu.VMEM((LAT, NSPAN * SPAN), jnp.bfloat16),
            pltpu.VMEM((2 * NX, LAT + 16, HEADS * SPAN), jnp.bfloat16),
            pltpu.SMEM((2 * NX,), jnp.int32),
        ],
        compiler_params=pltpu.CompilerParams(vmem_limit_bytes=VMEM_LIMIT),
    )(spans, query, own, other, turned_value)


def project_kernel(parts_ref, weight_ref, send_ref, keep_ref):
    c = lax.axis_index("c")
    heads = []
    packed = [parts_ref[i, HEADS * VD :, :].astype(jnp.float32) for i in range(NX)]
    for h in range(HEADS):
        logs = [(p[h : h + 1] + p[HEADS + h : HEADS + h + 1]) + p[2 * HEADS + h : 2 * HEADS + h + 1] for p in packed]
        highest = functools.reduce(jnp.maximum, logs)
        shares = [jnp.exp2(v - highest) for v in logs]
        inverse = 1.0 / functools.reduce(jnp.add, shares)
        merged = functools.reduce(
            jnp.add,
            [
                (shares[i] * inverse) * parts_ref[i, h * VD : (h + 1) * VD, :].astype(jnp.float32)
                for i in range(NX)
            ],
        )
        heads.append(merged.T.astype(jnp.bfloat16))
    head_out = jnp.concatenate(heads, axis=1)
    step = weight_ref.shape[1] // NY
    width = step // (NZH * NC)
    for y in range(NY):
        result = jnp.dot(
            head_out, weight_ref[:, y * step : (y + 1) * step], preferred_element_type=jnp.float32
        ).T.astype(jnp.bfloat16)
        for zh in range(NZH):
            even = result[2 * zh * width : (2 * zh + 1) * width]
            odd = result[(2 * zh + 1) * width : (2 * zh + 2) * width]
            keep_ref[y, zh] = jnp.where(c == 0, even, odd)
            send_ref[y, zh] = jnp.where(c == 0, odd, even)


def project(parts, weight):
    width = weight.shape[1] // (NY * NZH * NC)
    piece = jax.ShapeDtypeStruct((NY, NZH, width, 2 * SPAN), jnp.bfloat16)
    return pl.pallas_call(
        project_kernel,
        out_shape=(piece, piece),
        in_specs=[WHOLE, WHOLE],
        out_specs=(WHOLE, WHOLE),
        compiler_params=pltpu.CompilerParams(vmem_limit_bytes=VMEM_LIMIT),
    )(parts, weight)


def swapped(value, axis):
    return lax.ppermute(value, axis, [(0, 1), (1, 0)])


def exchanged(value, axis):
    return lax.all_to_all(value, axis, split_axis=0, concat_axis=0, tiled=True)


def on_device(query_plain, query_rotary, latent_keys, span_order, key_up, value_up, output_weight):
    zh = lax.axis_index("zh")
    tables = jnp.asarray(rotary_tables())
    sent_keys = pl.pallas_call(
        keys_kernel,
        out_shape=jax.ShapeDtypeStruct((GROUP, 8, ROWW), jnp.bfloat16),
        in_specs=[SMEM, WHOLE, WHOLE],
        out_specs=WHOLE,
    )(span_order, latent_keys, tables)
    rows = jax.ShapeDtypeStruct((2 * SPAN, QW), jnp.bfloat16)
    queries, kept_spans = pl.pallas_call(
        queries_kernel,
        out_shape=(rows, jax.ShapeDtypeStruct(span_order.shape, span_order.dtype)),
        in_specs=[SMEM, WHOLE, WHOLE, WHOLE, pl.BlockSpec(memory_space=pl.ANY)],
        out_specs=(WHOLE, SMEM),
    )(span_order, query_plain, query_rotary, tables, sent_keys)
    along_z = exchanged(sent_keys, ("zl", "zh")).reshape(GROUP * 8, ROWW)
    blocks = [queries] + [
        lax.ppermute(queries, "x", [(i, (i + k) % NX) for i in range(NX)]) for k in range(1, NX)
    ]
    along_z, blocks[1], blocks[3] = lax.optimization_barrier((along_z, blocks[1], blocks[3]))
    own = exchanged(jnp.broadcast_to(along_z[None], (NY, GROUP * 8, ROWW)), "y").reshape(NY * GROUP * 8, ROWW)
    own, blocks[2] = lax.optimization_barrier((own, blocks[2]))
    other = swapped(own, "c")
    query, turned_value = absorb(blocks, key_up, value_up)
    parts = attend(kept_spans, query, own, other, turned_value)
    send, keep = project(exchanged(parts, "x"), output_weight)
    both = (keep.astype(jnp.float32) + swapped(send, "c").astype(jnp.float32)).astype(jnp.bfloat16)
    over_y = exchanged(both, "y").astype(jnp.float32)
    mine = jnp.sum(lax.dynamic_index_in_dim(over_y, zh, 1, keepdims=False), axis=0)
    theirs = jnp.sum(lax.dynamic_index_in_dim(over_y, 1 - zh, 1, keepdims=False), axis=0).astype(jnp.bfloat16)
    return (mine + swapped(theirs, "zh").astype(jnp.float32)).astype(jnp.bfloat16).T


def solution(mesh):
    finer = Mesh(
        mesh.devices.reshape(NZL, NX, NY, NZH, NC), ("zl", "x", "y", "zh", "c")
    )
    in_specs = (
        P(CTX, TP),
        P(CTX, TP),
        P(CTX + TP, None),
        P(),
        P(TP, None, None),
        P(TP, None, None),
        P(TP, None),
    )
    return jax.shard_map(
        on_device, mesh=finer, in_specs=in_specs, out_specs=P(CTX, TP), check_vma=False
    )
```

```python
import functools
import math

import jax
import jax.numpy as jnp
import numpy as np
from jax import lax
from jax.experimental import pallas as pl
from jax.experimental.pallas import tpu as pltpu
from jax.sharding import Mesh
from jax.sharding import PartitionSpec as P

NZL, NX, NY, NZH, NC = 8, 4, 4, 2, 2
CTX = ("zl", "x")
TP = ("y", "zh", "c")

SPAN = 64
ROPE = 64
LAT = 512
NOPE = 128
VD = 128
HEADS = 4
KEYW = LAT + ROPE
ROWW = 640
GROUP = NZL * NZH
NSPAN = 2 * NZL
CHUNK = 256
GROUPED = 4
QW = HEADS * (NOPE + ROPE)
PARTROWS = HEADS * VD + 16
BASE = 10000.0
LOW = -1e30
SCALE = math.log2(math.e) / math.sqrt(NOPE + ROPE)
VMEM_LIMIT = 48 * 1024 * 1024


def rotary_tables():
    lane = np.arange(128)
    freq = BASE ** (-2.0 * (lane % 32) / ROPE)
    sign = np.where(lane % 64 < 32, -1.0, 1.0)
    start = (np.arange(64) * SPAN)[:, None] * freq[None, :]
    offset = np.arange(SPAN)[:, None] * freq[None, :]
    tables = [np.cos(start), sign * np.sin(start), np.cos(offset), sign * np.sin(offset)]
    return np.stack(tables).astype(np.float32)


def turn(values, cosine, signed_sine):
    lane = lax.broadcasted_iota(jnp.int32, values.shape, 1)
    partner = jnp.where(
        lane % 64 < 32, pltpu.roll(values, 96, axis=1), pltpu.roll(values, 32, axis=1)
    )
    return values * cosine + partner * signed_sine


def angle_of(tables_ref, span, offset_rows):
    cos_a = tables_ref[0, pl.ds(span, 1), :]
    sin_a = tables_ref[1, pl.ds(span, 1), :]
    cos_b = tables_ref[2, offset_rows, :]
    sin_b = tables_ref[3, offset_rows, :]
    return cos_a * cos_b - sin_a * sin_b, sin_a * cos_b + cos_a * sin_b


def own_ctx():
    return lax.axis_index("zl") * NX + lax.axis_index("x")


def own_tp():
    return (lax.axis_index("y") * NZH + lax.axis_index("zh")) * NC + lax.axis_index("c")


def keys_kernel(spans_ref, keys_ref, tables_ref, out_ref):
    tp = own_tp()
    span = spans_ref[own_ctx() * 2 + tp // 8]
    first = pl.multiple_of((tp % 8) * 8, 8)
    cosine, sine = angle_of(tables_ref, span, pl.ds(first, 8))
    tail = keys_ref[:, LAT:].astype(jnp.float32)
    turned = turn(jnp.concatenate([tail, tail], axis=1), cosine, sine).astype(jnp.bfloat16)
    for k in range(GROUP):
        out_ref[k, :, :LAT] = keys_ref[:, :LAT]
        out_ref[k, :, LAT:] = turned


def queries_kernel(spans_ref, plain_ref, rotary_ref, tables_ref, after_ref, out_ref, kept_spans_ref):
    out_ref[:, : HEADS * NOPE] = plain_ref[...]
    for s in range(2):
        rows = slice(s * SPAN, (s + 1) * SPAN)
        cosine, sine = angle_of(tables_ref, spans_ref[own_ctx() * 2 + s], pl.ds(0, SPAN))
        for j in range(HEADS * ROPE // 128):
            part = rotary_ref[rows, j * 128 : (j + 1) * 128].astype(jnp.float32)
            at = HEADS * NOPE + j * 128
            out_ref[rows, at : at + 128] = (turn(part, cosine, sine) * SCALE).astype(jnp.bfloat16)
    for i in range(kept_spans_ref.shape[0]):
        kept_spans_ref[i] = spans_ref[i]


SMEM = pl.BlockSpec(memory_space=pltpu.SMEM)
WHOLE = pl.BlockSpec(memory_space=pltpu.VMEM)
HBM = pl.BlockSpec(memory_space=pltpu.HBM)


def absorb_kernel(q0_hbm, q1, q2, q3, up_hbm, value_hbm, query, turned_value, q0, up_ref, value_ref, arrived):
    fetches = [
        pltpu.make_async_copy(source, target, arrived.at[i])
        for i, (source, target) in enumerate(((q0_hbm, q0), (up_hbm, up_ref), (value_hbm, value_ref)))
    ]
    for fetch in fetches:
        fetch.start()
    for fetch in fetches:
        fetch.wait()
    blocks = (q0, q1, q2, q3)
    for h in range(HEADS):
        plain = jnp.concatenate([block[:, h * NOPE : (h + 1) * NOPE] for block in blocks], axis=0)
        absorbed = (jnp.dot(plain, up_ref[h], preferred_element_type=jnp.float32) * SCALE).astype(jnp.bfloat16)
        first = HEADS * NOPE + h * ROPE
        at = slice(h * SPAN, (h + 1) * SPAN)
        for b in range(2 * NX):
            query[b, at, :LAT] = absorbed[b * SPAN : (b + 1) * SPAN]
            query[b, at, LAT:] = blocks[b // 2][(b % 2) * SPAN : (b % 2 + 1) * SPAN, first : first + ROPE]
    for h in range(HEADS):
        turned_value[h] = value_ref[h].T


def in_hbm(value):
    return pltpu.with_memory_space_constraint(value, pltpu.HBM)


def absorb(blocks, key_up, value_up):
    return pl.pallas_call(
        absorb_kernel,
        out_shape=(
            jax.ShapeDtypeStruct((2 * NX, HEADS * SPAN, KEYW), jnp.bfloat16),
            jax.ShapeDtypeStruct((HEADS, VD, LAT), jnp.bfloat16),
        ),
        in_specs=[HBM] + [WHOLE] * 3 + [HBM] * 2,
        out_specs=(WHOLE, WHOLE),
        scratch_shapes=[
            pltpu.VMEM(blocks[0].shape, jnp.bfloat16),
            pltpu.VMEM(key_up.shape, jnp.bfloat16),
            pltpu.VMEM(value_up.shape, jnp.bfloat16),
            pltpu.SemaphoreType.DMA((3,)),
        ],
        compiler_params=pltpu.CompilerParams(vmem_limit_bytes=VMEM_LIMIT),
    )(in_hbm(blocks[0]), *blocks[1:], in_hbm(key_up), in_hbm(value_up))


def attend_kernel(
    spans_ref, query, own_ref, other_ref, value_ref, out_ref, sorted_keys, latent, contexts, order
):
    zl = lax.axis_index("zl")
    x = lax.axis_index("x")
    c = lax.axis_index("c")

    places = [spans_ref[((i // 2) * NX + x) * 2 + i % 2] for i in range(NSPAN)]

    def earlier(place, among):
        return functools.reduce(jnp.add, [(p < place).astype(jnp.int32) for p in among])

    for i in range(NSPAN):
        rank = earlier(places[i], places)
        for half, keys in enumerate((own_ref, other_ref)):
            for low in range(2):
                source = ((i % 2) * 2 + low) * GROUP * 8 + (i // 2) * NZH * 8
                target = pl.multiple_of(rank * SPAN + half * 32 + low * 16, 16)
                sorted_keys[pl.ds(target, 16), :] = keys[source : source + 16, :]

    asking = [spans_ref[(zl * NX + (x + NX - b // 2) % NX) * 2 + b % 2] for b in range(2 * NX)]
    for b in range(2 * NX):
        order[earlier(asking[b], asking)] = b

    for n in range(NSPAN * SPAN // CHUNK):
        at = slice(n * CHUNK, (n + 1) * CHUNK)
        latent[:, at] = sorted_keys[at, :LAT].T

    row = lax.broadcasted_iota(jnp.int32, (CHUNK, HEADS * SPAN), 0)
    core = jnp.where(row // 32 % 2 == 0, c, 1 - c)
    key_order = row // SPAN * SPAN + row // 16 % 2 * 32 + row // 8 % 2 * 16 + core * 8 + row % 8
    token = lax.broadcasted_iota(jnp.int32, (1, HEADS * SPAN), 1) % SPAN
    head = lax.broadcasted_iota(jnp.int32, (16, HEADS * SPAN), 1) // SPAN
    dims = (((1,), (1,)), ((), ()))

    def some_spans(turn_of, carry):
        spans = [order[GROUPED * turn_of + i] for i in range(GROUPED)]
        limits = []
        for b in spans:
            source = (x + NX - b // 2) % NX
            below = earlier(spans_ref[(zl * NX + source) * 2 + b % 2], places)
            limits.append(below * SPAN + jnp.where(source == x, token, -1))
            needed = below + (source == x).astype(jnp.int32)
        chunks = jnp.maximum((needed + CHUNK // SPAN - 1) // (CHUNK // SPAN), 1)

        for count in range(1, NSPAN * SPAN // CHUNK + 1):

            @pl.when(chunks == count)
            def _(count=count):
                products = [
                    [
                        lax.dot_general(
                            sorted_keys[n * CHUNK : (n + 1) * CHUNK, :KEYW],
                            query[b],
                            dims,
                            preferred_element_type=jnp.float32,
                        )
                        for n in range(count)
                    ]
                    for b in spans
                ]
                for b, limit, scores in zip(spans, limits, products):
                    scores = [
                        jnp.where(key_order <= limit - n * CHUNK, score, LOW) for n, score in enumerate(scores)
                    ]
                    highest = functools.reduce(jnp.maximum, [jnp.max(v, axis=0, keepdims=True) for v in scores])
                    raised = [jnp.exp2(score - highest) for score in scores]
                    total = functools.reduce(jnp.add, [jnp.sum(v, axis=0, keepdims=True) for v in raised])
                    context = jnp.dot(
                        latent[:, : count * CHUNK],
                        jnp.concatenate([v.astype(jnp.bfloat16) for v in raised], axis=0),
                        preferred_element_type=jnp.float32,
                    )
                    contexts[b, :LAT, :] = (context * (1.0 / total)).astype(jnp.bfloat16)
                    log_sum = highest + jnp.log2(total)
                    high = log_sum.astype(jnp.bfloat16).astype(jnp.float32)
                    rest = log_sum - high
                    middle = rest.astype(jnp.bfloat16).astype(jnp.float32)
                    place = lax.broadcasted_iota(jnp.int32, (16, HEADS * SPAN), 0)
                    packed = jnp.where(place < HEADS, high, jnp.where(place < 2 * HEADS, middle, rest - middle))
                    packed = jnp.where((place < 3 * HEADS) & (place % HEADS == head), packed, 0.0)
                    contexts[b, LAT:, :] = packed.astype(jnp.bfloat16)

        return carry

    lax.fori_loop(0, 2 * NX // GROUPED, some_spans, 0)

    for h in range(HEADS):
        at = slice(h * SPAN, (h + 1) * SPAN)
        joined = jnp.concatenate([contexts[b, :LAT, at] for b in range(2 * NX)], axis=1)
        values = jnp.dot(value_ref[h], joined, preferred_element_type=jnp.float32).astype(jnp.bfloat16)
        for k in range(NX):
            tokens = slice(k * 2 * SPAN, (k + 1) * 2 * SPAN)
            out_ref[(x + NX - k) % NX, h * VD : (h + 1) * VD, :] = values[:, tokens]
    for k in range(NX):
        logs = [
            functools.reduce(
                jnp.add,
                [
                    contexts[b, LAT:, h * SPAN : (h + 1) * SPAN].astype(jnp.float32)
                    for h in range(HEADS)
                ],
            )
            for b in (2 * k, 2 * k + 1)
        ]
        out_ref[(x + NX - k) % NX, HEADS * VD :, :] = jnp.concatenate(logs, axis=1).astype(jnp.bfloat16)


def attend(spans, query, own, other, turned_value):
    return pl.pallas_call(
        attend_kernel,
        out_shape=jax.ShapeDtypeStruct((NX, PARTROWS, 2 * SPAN), jnp.bfloat16),
        in_specs=[SMEM] + [WHOLE] * 4,
        out_specs=WHOLE,
        scratch_shapes=[
            pltpu.VMEM((NSPAN * SPAN, ROWW), jnp.bfloat16),
            pltpu.VMEM((LAT, NSPAN * SPAN), jnp.bfloat16),
            pltpu.VMEM((2 * NX, LAT + 16, HEADS * SPAN), jnp.bfloat16),
            pltpu.SMEM((2 * NX,), jnp.int32),
        ],
        compiler_params=pltpu.CompilerParams(vmem_limit_bytes=VMEM_LIMIT),
    )(spans, query, own, other, turned_value)


def project_kernel(parts_ref, weight_ref, send_ref, keep_ref):
    c = lax.axis_index("c")
    heads = []
    packed = [parts_ref[i, HEADS * VD :, :].astype(jnp.float32) for i in range(NX)]
    for h in range(HEADS):
        logs = [(p[h : h + 1] + p[HEADS + h : HEADS + h + 1]) + p[2 * HEADS + h : 2 * HEADS + h + 1] for p in packed]
        highest = functools.reduce(jnp.maximum, logs)
        shares = [jnp.exp2(v - highest) for v in logs]
        inverse = 1.0 / functools.reduce(jnp.add, shares)
        merged = functools.reduce(
            jnp.add,
            [
                (shares[i] * inverse) * parts_ref[i, h * VD : (h + 1) * VD, :].astype(jnp.float32)
                for i in range(NX)
            ],
        )
        heads.append(merged.T.astype(jnp.bfloat16))
    head_out = jnp.concatenate(heads, axis=1)
    step = weight_ref.shape[1] // NY
    width = step // (NZH * NC)
    for y in range(NY):
        result = jnp.dot(
            head_out, weight_ref[:, y * step : (y + 1) * step], preferred_element_type=jnp.float32
        ).T.astype(jnp.bfloat16)
        for zh in range(NZH):
            even = result[2 * zh * width : (2 * zh + 1) * width]
            odd = result[(2 * zh + 1) * width : (2 * zh + 2) * width]
            keep_ref[y, zh] = jnp.where(c == 0, even, odd)
            send_ref[y, zh] = jnp.where(c == 0, odd, even)


def project(parts, weight):
    width = weight.shape[1] // (NY * NZH * NC)
    piece = jax.ShapeDtypeStruct((NY, NZH, width, 2 * SPAN), jnp.bfloat16)
    return pl.pallas_call(
        project_kernel,
        out_shape=(piece, piece),
        in_specs=[WHOLE, WHOLE],
        out_specs=(WHOLE, WHOLE),
        compiler_params=pltpu.CompilerParams(vmem_limit_bytes=VMEM_LIMIT),
    )(parts, weight)


def swapped(value, axis):
    return lax.ppermute(value, axis, [(0, 1), (1, 0)])


def exchanged(value, axis):
    return lax.all_to_all(value, axis, split_axis=0, concat_axis=0, tiled=True)


def on_device(query_plain, query_rotary, latent_keys, span_order, key_up, value_up, output_weight):
    tables = jnp.asarray(rotary_tables())
    sent_keys = pl.pallas_call(
        keys_kernel,
        out_shape=jax.ShapeDtypeStruct((GROUP, 8, ROWW), jnp.bfloat16),
        in_specs=[SMEM, WHOLE, WHOLE],
        out_specs=WHOLE,
    )(span_order, latent_keys, tables)
    rows = jax.ShapeDtypeStruct((2 * SPAN, QW), jnp.bfloat16)
    queries, kept_spans = pl.pallas_call(
        queries_kernel,
        out_shape=(rows, jax.ShapeDtypeStruct(span_order.shape, span_order.dtype)),
        in_specs=[SMEM, WHOLE, WHOLE, WHOLE, pl.BlockSpec(memory_space=pl.ANY)],
        out_specs=(WHOLE, SMEM),
    )(span_order, query_plain, query_rotary, tables, sent_keys)
    along_z = exchanged(sent_keys, ("zl", "zh")).reshape(GROUP * 8, ROWW)
    blocks = [queries] + [
        lax.ppermute(queries, "x", [(i, (i + k) % NX) for i in range(NX)]) for k in range(1, NX)
    ]
    along_z, blocks[1], blocks[3] = lax.optimization_barrier((along_z, blocks[1], blocks[3]))
    own = exchanged(jnp.broadcast_to(along_z[None], (NY, GROUP * 8, ROWW)), "y").reshape(NY * GROUP * 8, ROWW)
    own, blocks[2] = lax.optimization_barrier((own, blocks[2]))
    other = swapped(own, "c")
    query, turned_value = absorb(blocks, key_up, value_up)
    parts = attend(kept_spans, query, own, other, turned_value)
    send, keep = project(exchanged(parts, "x"), output_weight)
    both = (keep.astype(jnp.float32) + swapped(send, "c").astype(jnp.float32)).astype(jnp.bfloat16)
    pieces = exchanged(both.reshape(NY * NZH, *both.shape[2:]), ("y", "zh"))
    return jnp.sum(pieces.astype(jnp.float32), axis=0).astype(jnp.bfloat16).T


def solution(mesh):
    finer = Mesh(
        mesh.devices.reshape(NZL, NX, NY, NZH, NC), ("zl", "x", "y", "zh", "c")
    )
    in_specs = (
        P(CTX, TP),
        P(CTX, TP),
        P(CTX + TP, None),
        P(),
        P(TP, None, None),
        P(TP, None, None),
        P(TP, None),
    )
    return jax.shard_map(
        on_device, mesh=finer, in_specs=in_specs, out_specs=P(CTX, TP), check_vma=False
    )
```

```python
import functools
import math

import jax
import jax.numpy as jnp
import numpy as np
from jax import lax
from jax.experimental import pallas as pl
from jax.experimental.pallas import tpu as pltpu
from jax.sharding import Mesh
from jax.sharding import PartitionSpec as P

NZL, NX, NY, NZH, NC = 8, 4, 4, 2, 2
CTX = ("zl", "x")
TP = ("y", "zh", "c")

SPAN = 64
ROPE = 64
LAT = 512
NOPE = 128
VD = 128
HEADS = 4
KEYW = LAT + ROPE
ROWW = 640
GROUP = NZL * NZH
NSPAN = 2 * NZL
CHUNK = 256
GROUPED = 4
QW = HEADS * (NOPE + ROPE)
PARTROWS = HEADS * VD + 16
BASE = 10000.0
LOW = -1e30
SCALE = math.log2(math.e) / math.sqrt(NOPE + ROPE)
VMEM_LIMIT = 48 * 1024 * 1024


def rotary_tables():
    lane = np.arange(128)
    freq = BASE ** (-2.0 * (lane % 32) / ROPE)
    sign = np.where(lane % 64 < 32, -1.0, 1.0)
    start = (np.arange(64) * SPAN)[:, None] * freq[None, :]
    offset = np.arange(SPAN)[:, None] * freq[None, :]
    tables = [np.cos(start), sign * np.sin(start), np.cos(offset), sign * np.sin(offset)]
    return np.stack(tables).astype(np.float32)


def turn(values, cosine, signed_sine):
    lane = lax.broadcasted_iota(jnp.int32, values.shape, 1)
    partner = jnp.where(
        lane % 64 < 32, pltpu.roll(values, 96, axis=1), pltpu.roll(values, 32, axis=1)
    )
    return values * cosine + partner * signed_sine


def angle_of(tables_ref, span, offset_rows):
    cos_a = tables_ref[0, pl.ds(span, 1), :]
    sin_a = tables_ref[1, pl.ds(span, 1), :]
    cos_b = tables_ref[2, offset_rows, :]
    sin_b = tables_ref[3, offset_rows, :]
    return cos_a * cos_b - sin_a * sin_b, sin_a * cos_b + cos_a * sin_b


def own_ctx():
    return lax.axis_index("zl") * NX + lax.axis_index("x")


def own_tp():
    return (lax.axis_index("y") * NZH + lax.axis_index("zh")) * NC + lax.axis_index("c")


def keys_kernel(spans_ref, keys_ref, tables_ref, out_ref):
    tp = own_tp()
    span = spans_ref[own_ctx() * 2 + tp // 8]
    first = pl.multiple_of((tp % 8) * 8, 8)
    cosine, sine = angle_of(tables_ref, span, pl.ds(first, 8))
    tail = keys_ref[:, LAT:].astype(jnp.float32)
    turned = turn(jnp.concatenate([tail, tail], axis=1), cosine, sine).astype(jnp.bfloat16)
    for k in range(GROUP):
        out_ref[k, :, :LAT] = keys_ref[:, :LAT]
        out_ref[k, :, LAT:] = turned


def queries_kernel(spans_ref, plain_ref, rotary_ref, tables_ref, after_ref, out_ref, kept_spans_ref):
    out_ref[:, : HEADS * NOPE] = plain_ref[...]
    for s in range(2):
        rows = slice(s * SPAN, (s + 1) * SPAN)
        cosine, sine = angle_of(tables_ref, spans_ref[own_ctx() * 2 + s], pl.ds(0, SPAN))
        for j in range(HEADS * ROPE // 128):
            part = rotary_ref[rows, j * 128 : (j + 1) * 128].astype(jnp.float32)
            at = HEADS * NOPE + j * 128
            out_ref[rows, at : at + 128] = (turn(part, cosine, sine) * SCALE).astype(jnp.bfloat16)
    for i in range(kept_spans_ref.shape[0]):
        kept_spans_ref[i] = spans_ref[i]


SMEM = pl.BlockSpec(memory_space=pltpu.SMEM)
WHOLE = pl.BlockSpec(memory_space=pltpu.VMEM)
HBM = pl.BlockSpec(memory_space=pltpu.HBM)


def absorb_kernel(q0_hbm, q1, q2, q3, up_hbm, value_hbm, query, turned_value, q0, up_ref, value_ref, arrived):
    fetches = [
        pltpu.make_async_copy(source, target, arrived.at[i])
        for i, (source, target) in enumerate(((q0_hbm, q0), (up_hbm, up_ref), (value_hbm, value_ref)))
    ]
    for fetch in fetches:
        fetch.start()
    for fetch in fetches:
        fetch.wait()
    blocks = (q0, q1, q2, q3)
    for h in range(HEADS):
        plain = jnp.concatenate([block[:, h * NOPE : (h + 1) * NOPE] for block in blocks], axis=0)
        absorbed = (jnp.dot(plain, up_ref[h], preferred_element_type=jnp.float32) * SCALE).astype(jnp.bfloat16)
        first = HEADS * NOPE + h * ROPE
        at = slice(h * SPAN, (h + 1) * SPAN)
        for b in range(2 * NX):
            query[b, at, :LAT] = absorbed[b * SPAN : (b + 1) * SPAN]
            query[b, at, LAT:] = blocks[b // 2][(b % 2) * SPAN : (b % 2 + 1) * SPAN, first : first + ROPE]
    for h in range(HEADS):
        turned_value[h] = value_ref[h].T


def in_hbm(value):
    return pltpu.with_memory_space_constraint(value, pltpu.HBM)


def absorb(blocks, key_up, value_up):
    return pl.pallas_call(
        absorb_kernel,
        out_shape=(
            jax.ShapeDtypeStruct((2 * NX, HEADS * SPAN, KEYW), jnp.bfloat16),
            jax.ShapeDtypeStruct((HEADS, VD, LAT), jnp.bfloat16),
        ),
        in_specs=[HBM] + [WHOLE] * 3 + [HBM] * 2,
        out_specs=(WHOLE, WHOLE),
        scratch_shapes=[
            pltpu.VMEM(blocks[0].shape, jnp.bfloat16),
            pltpu.VMEM(key_up.shape, jnp.bfloat16),
            pltpu.VMEM(value_up.shape, jnp.bfloat16),
            pltpu.SemaphoreType.DMA((3,)),
        ],
        compiler_params=pltpu.CompilerParams(vmem_limit_bytes=VMEM_LIMIT),
    )(in_hbm(blocks[0]), *blocks[1:], in_hbm(key_up), in_hbm(value_up))


def attend_kernel(
    spans_ref, query, own_ref, other_ref, value_ref, out_ref, sorted_keys, latent, contexts, order
):
    zl = lax.axis_index("zl")
    x = lax.axis_index("x")
    c = lax.axis_index("c")

    places = [spans_ref[((i // 2) * NX + x) * 2 + i % 2] for i in range(NSPAN)]

    def earlier(place, among):
        return functools.reduce(jnp.add, [(p < place).astype(jnp.int32) for p in among])

    for i in range(NSPAN):
        rank = earlier(places[i], places)
        for half, keys in enumerate((own_ref, other_ref)):
            for low in range(2):
                source = ((i % 2) * 2 + low) * GROUP * 8 + (i // 2) * NZH * 8
                target = pl.multiple_of(rank * SPAN + half * 32 + low * 16, 16)
                sorted_keys[pl.ds(target, 16), :] = keys[source : source + 16, :]

    asking = [spans_ref[(zl * NX + (x + NX - b // 2) % NX) * 2 + b % 2] for b in range(2 * NX)]
    for b in range(2 * NX):
        order[earlier(asking[b], asking)] = b

    for n in range(NSPAN * SPAN // CHUNK):
        at = slice(n * CHUNK, (n + 1) * CHUNK)
        latent[:, at] = sorted_keys[at, :LAT].T

    row = lax.broadcasted_iota(jnp.int32, (CHUNK, HEADS * SPAN), 0)
    core = jnp.where(row // 32 % 2 == 0, c, 1 - c)
    key_order = row // SPAN * SPAN + row // 16 % 2 * 32 + row // 8 % 2 * 16 + core * 8 + row % 8
    token = lax.broadcasted_iota(jnp.int32, (1, HEADS * SPAN), 1) % SPAN
    head = lax.broadcasted_iota(jnp.int32, (16, HEADS * SPAN), 1) // SPAN
    dims = (((1,), (1,)), ((), ()))

    def some_spans(turn_of, carry):
        spans = [order[GROUPED * turn_of + i] for i in range(GROUPED)]
        limits = []
        for b in spans:
            source = (x + NX - b // 2) % NX
            below = earlier(spans_ref[(zl * NX + source) * 2 + b % 2], places)
            limits.append(below * SPAN + jnp.where(source == x, token, -1))
            needed = below + (source == x).astype(jnp.int32)
        chunks = jnp.maximum((needed + CHUNK // SPAN - 1) // (CHUNK // SPAN), 1)

        for count in range(1, NSPAN * SPAN // CHUNK + 1):

            @pl.when(chunks == count)
            def _(count=count):
                products = [
                    [
                        lax.dot_general(
                            sorted_keys[n * CHUNK : (n + 1) * CHUNK, :KEYW],
                            query[b],
                            dims,
                            preferred_element_type=jnp.float32,
                        )
                        for n in range(count)
                    ]
                    for b in spans
                ]
                for b, limit, scores in zip(spans, limits, products):
                    scores = [
                        jnp.where(key_order <= limit - n * CHUNK, score, LOW) for n, score in enumerate(scores)
                    ]
                    highest = functools.reduce(jnp.maximum, [jnp.max(v, axis=0, keepdims=True) for v in scores])
                    raised = [jnp.exp2(score - highest) for score in scores]
                    total = functools.reduce(jnp.add, [jnp.sum(v, axis=0, keepdims=True) for v in raised])
                    context = jnp.dot(
                        latent[:, : count * CHUNK],
                        jnp.concatenate([v.astype(jnp.bfloat16) for v in raised], axis=0),
                        preferred_element_type=jnp.float32,
                    )
                    contexts[b, :LAT, :] = (context * (1.0 / total)).astype(jnp.bfloat16)
                    log_sum = highest + jnp.log2(total)
                    high = log_sum.astype(jnp.bfloat16).astype(jnp.float32)
                    rest = log_sum - high
                    middle = rest.astype(jnp.bfloat16).astype(jnp.float32)
                    place = lax.broadcasted_iota(jnp.int32, (16, HEADS * SPAN), 0)
                    packed = jnp.where(place < HEADS, high, jnp.where(place < 2 * HEADS, middle, rest - middle))
                    packed = jnp.where((place < 3 * HEADS) & (place % HEADS == head), packed, 0.0)
                    contexts[b, LAT:, :] = packed.astype(jnp.bfloat16)

        return carry

    lax.fori_loop(0, 2 * NX // GROUPED, some_spans, 0)

    for h in range(HEADS):
        at = slice(h * SPAN, (h + 1) * SPAN)
        joined = jnp.concatenate([contexts[b, :LAT, at] for b in range(2 * NX)], axis=1)
        values = jnp.dot(value_ref[h], joined, preferred_element_type=jnp.float32).astype(jnp.bfloat16)
        for k in range(NX):
            tokens = slice(k * 2 * SPAN, (k + 1) * 2 * SPAN)
            out_ref[(x + NX - k) % NX, h * VD : (h + 1) * VD, :] = values[:, tokens]
    for k in range(NX):
        logs = [
            functools.reduce(
                jnp.add,
                [
                    contexts[b, LAT:, h * SPAN : (h + 1) * SPAN].astype(jnp.float32)
                    for h in range(HEADS)
                ],
            )
            for b in (2 * k, 2 * k + 1)
        ]
        out_ref[(x + NX - k) % NX, HEADS * VD :, :] = jnp.concatenate(logs, axis=1).astype(jnp.bfloat16)


def attend(spans, query, own, other, turned_value):
    return pl.pallas_call(
        attend_kernel,
        out_shape=jax.ShapeDtypeStruct((NX, PARTROWS, 2 * SPAN), jnp.bfloat16),
        in_specs=[SMEM] + [WHOLE] * 4,
        out_specs=WHOLE,
        scratch_shapes=[
            pltpu.VMEM((NSPAN * SPAN, ROWW), jnp.bfloat16),
            pltpu.VMEM((LAT, NSPAN * SPAN), jnp.bfloat16),
            pltpu.VMEM((2 * NX, LAT + 16, HEADS * SPAN), jnp.bfloat16),
            pltpu.SMEM((2 * NX,), jnp.int32),
        ],
        compiler_params=pltpu.CompilerParams(vmem_limit_bytes=VMEM_LIMIT),
    )(spans, query, own, other, turned_value)


def project_kernel(parts_ref, weight_ref, send_ref, keep_ref):
    c = lax.axis_index("c")
    heads = []
    packed = [parts_ref[i, HEADS * VD :, :].astype(jnp.float32) for i in range(NX)]
    for h in range(HEADS):
        logs = [(p[h : h + 1] + p[HEADS + h : HEADS + h + 1]) + p[2 * HEADS + h : 2 * HEADS + h + 1] for p in packed]
        highest = functools.reduce(jnp.maximum, logs)
        shares = [jnp.exp2(v - highest) for v in logs]
        inverse = 1.0 / functools.reduce(jnp.add, shares)
        merged = functools.reduce(
            jnp.add,
            [
                (shares[i] * inverse) * parts_ref[i, h * VD : (h + 1) * VD, :].astype(jnp.float32)
                for i in range(NX)
            ],
        )
        heads.append(merged.T.astype(jnp.bfloat16))
    head_out = jnp.concatenate(heads, axis=1)
    step = weight_ref.shape[1] // NY
    width = step // (NZH * NC)
    for y in range(NY):
        result = jnp.dot(
            head_out, weight_ref[:, y * step : (y + 1) * step], preferred_element_type=jnp.float32
        ).T.astype(jnp.bfloat16)
        for zh in range(NZH):
            even = result[2 * zh * width : (2 * zh + 1) * width]
            odd = result[(2 * zh + 1) * width : (2 * zh + 2) * width]
            keep_ref[y, zh] = jnp.where(c == 0, even, odd)
            send_ref[y, zh] = jnp.where(c == 0, odd, even)


def project(parts, weight):
    width = weight.shape[1] // (NY * NZH * NC)
    piece = jax.ShapeDtypeStruct((NY, NZH, width, 2 * SPAN), jnp.bfloat16)
    return pl.pallas_call(
        project_kernel,
        out_shape=(piece, piece),
        in_specs=[WHOLE, WHOLE],
        out_specs=(WHOLE, WHOLE),
        compiler_params=pltpu.CompilerParams(vmem_limit_bytes=VMEM_LIMIT),
    )(parts, weight)


def shifted(value, by):
    return lax.ppermute(value, "x", [(i, (i + by) % NX) for i in range(NX)])


def swapped(value, axis):
    return lax.ppermute(value, axis, [(0, 1), (1, 0)])


def exchanged(value, axis):
    return lax.all_to_all(value, axis, split_axis=0, concat_axis=0, tiled=True)


def on_device(query_plain, query_rotary, latent_keys, span_order, key_up, value_up, output_weight):
    zh = lax.axis_index("zh")
    tables = jnp.asarray(rotary_tables())
    sent_keys = pl.pallas_call(
        keys_kernel,
        out_shape=jax.ShapeDtypeStruct((GROUP, 8, ROWW), jnp.bfloat16),
        in_specs=[SMEM, WHOLE, WHOLE],
        out_specs=WHOLE,
    )(span_order, latent_keys, tables)
    rows = jax.ShapeDtypeStruct((2 * SPAN, QW), jnp.bfloat16)
    queries, kept_spans = pl.pallas_call(
        queries_kernel,
        out_shape=(rows, jax.ShapeDtypeStruct(span_order.shape, span_order.dtype)),
        in_specs=[SMEM, WHOLE, WHOLE, WHOLE, pl.BlockSpec(memory_space=pl.ANY)],
        out_specs=(WHOLE, SMEM),
    )(span_order, query_plain, query_rotary, tables, sent_keys)
    along_z = exchanged(sent_keys, ("zl", "zh")).reshape(GROUP * 8, ROWW)
    blocks = [queries, shifted(queries, 1), None, shifted(queries, NX - 1)]
    along_z, blocks[1], blocks[3] = lax.optimization_barrier((along_z, blocks[1], blocks[3]))
    blocks[2] = shifted(blocks[1], 1)
    own = exchanged(jnp.broadcast_to(along_z[None], (NY, GROUP * 8, ROWW)), "y").reshape(NY * GROUP * 8, ROWW)
    own, blocks[2] = lax.optimization_barrier((own, blocks[2]))
    other = swapped(own, "c")
    query, turned_value = absorb(blocks, key_up, value_up)
    parts = attend(kept_spans, query, own, other, turned_value)
    send, keep = project(exchanged(parts, "x"), output_weight)
    both = (keep.astype(jnp.float32) + swapped(send, "c").astype(jnp.float32)).astype(jnp.bfloat16)
    over_y = exchanged(both, "y").astype(jnp.float32)
    mine = jnp.sum(lax.dynamic_index_in_dim(over_y, zh, 1, keepdims=False), axis=0)
    theirs = jnp.sum(lax.dynamic_index_in_dim(over_y, 1 - zh, 1, keepdims=False), axis=0).astype(jnp.bfloat16)
    return (mine + swapped(theirs, "zh").astype(jnp.float32)).astype(jnp.bfloat16).T


def solution(mesh):
    finer = Mesh(
        mesh.devices.reshape(NZL, NX, NY, NZH, NC), ("zl", "x", "y", "zh", "c")
    )
    in_specs = (
        P(CTX, TP),
        P(CTX, TP),
        P(CTX + TP, None),
        P(),
        P(TP, None, None),
        P(TP, None, None),
        P(TP, None),
    )
    return jax.shard_map(
        on_device, mesh=finer, in_specs=in_specs, out_specs=P(CTX, TP), check_vma=False
    )
```

```python
import functools
import math

import jax
import jax.numpy as jnp
import numpy as np
from jax import lax
from jax.experimental import pallas as pl
from jax.experimental.pallas import tpu as pltpu
from jax.sharding import Mesh
from jax.sharding import PartitionSpec as P

NZL, NX, NY, NZH, NC = 8, 4, 4, 2, 2
CTX = ("zl", "x")
TP = ("y", "zh", "c")

SPAN = 64
ROPE = 64
LAT = 512
NOPE = 128
VD = 128
HEADS = 4
KEYW = LAT + ROPE
ROWW = 640
GROUP = NZL * NZH
NSPAN = 2 * NZL
CHUNK = 256
GROUPED = 4
QW = HEADS * (NOPE + ROPE)
PARTROWS = HEADS * VD + 16
BASE = 10000.0
LOW = -1e30
SCALE = math.log2(math.e) / math.sqrt(NOPE + ROPE)
VMEM_LIMIT = 48 * 1024 * 1024


def rotary_tables():
    lane = np.arange(128)
    freq = BASE ** (-2.0 * (lane % 32) / ROPE)
    sign = np.where(lane % 64 < 32, -1.0, 1.0)
    start = (np.arange(64) * SPAN)[:, None] * freq[None, :]
    offset = np.arange(SPAN)[:, None] * freq[None, :]
    tables = [np.cos(start), sign * np.sin(start), np.cos(offset), sign * np.sin(offset)]
    return np.stack(tables).astype(np.float32)


def turn(values, cosine, signed_sine):
    lane = lax.broadcasted_iota(jnp.int32, values.shape, 1)
    partner = jnp.where(
        lane % 64 < 32, pltpu.roll(values, 96, axis=1), pltpu.roll(values, 32, axis=1)
    )
    return values * cosine + partner * signed_sine


def angle_of(tables_ref, span, offset_rows):
    cos_a = tables_ref[0, pl.ds(span, 1), :]
    sin_a = tables_ref[1, pl.ds(span, 1), :]
    cos_b = tables_ref[2, offset_rows, :]
    sin_b = tables_ref[3, offset_rows, :]
    return cos_a * cos_b - sin_a * sin_b, sin_a * cos_b + cos_a * sin_b


def own_ctx():
    return lax.axis_index("zl") * NX + lax.axis_index("x")


def own_tp():
    return (lax.axis_index("y") * NZH + lax.axis_index("zh")) * NC + lax.axis_index("c")


def keys_kernel(spans_ref, keys_ref, tables_ref, out_ref):
    tp = own_tp()
    span = spans_ref[own_ctx() * 2 + tp // 8]
    first = pl.multiple_of((tp % 8) * 8, 8)
    cosine, sine = angle_of(tables_ref, span, pl.ds(first, 8))
    tail = keys_ref[:, LAT:].astype(jnp.float32)
    turned = turn(jnp.concatenate([tail, tail], axis=1), cosine, sine).astype(jnp.bfloat16)
    for k in range(GROUP):
        out_ref[k, :, :LAT] = keys_ref[:, :LAT]
        out_ref[k, :, LAT:] = turned


def queries_kernel(spans_ref, plain_ref, rotary_ref, tables_ref, after_ref, out_ref, kept_spans_ref):
    out_ref[:, : HEADS * NOPE] = plain_ref[...]
    for s in range(2):
        rows = slice(s * SPAN, (s + 1) * SPAN)
        cosine, sine = angle_of(tables_ref, spans_ref[own_ctx() * 2 + s], pl.ds(0, SPAN))
        for j in range(HEADS * ROPE // 128):
            part = rotary_ref[rows, j * 128 : (j + 1) * 128].astype(jnp.float32)
            at = HEADS * NOPE + j * 128
            out_ref[rows, at : at + 128] = (turn(part, cosine, sine) * SCALE).astype(jnp.bfloat16)
    for i in range(kept_spans_ref.shape[0]):
        kept_spans_ref[i] = spans_ref[i]


SMEM = pl.BlockSpec(memory_space=pltpu.SMEM)
WHOLE = pl.BlockSpec(memory_space=pltpu.VMEM)
HBM = pl.BlockSpec(memory_space=pltpu.HBM)


def absorb_kernel(q0_hbm, q1, q2, q3, up_hbm, value_hbm, query, turned_value, q0, up_ref, value_ref, arrived):
    fetches = [
        pltpu.make_async_copy(source, target, arrived.at[i])
        for i, (source, target) in enumerate(((q0_hbm, q0), (up_hbm, up_ref), (value_hbm, value_ref)))
    ]
    for fetch in fetches:
        fetch.start()
    for fetch in fetches:
        fetch.wait()
    blocks = (q0, q1, q2, q3)
    for h in range(HEADS):
        plain = jnp.concatenate([block[:, h * NOPE : (h + 1) * NOPE] for block in blocks], axis=0)
        absorbed = (jnp.dot(plain, up_ref[h], preferred_element_type=jnp.float32) * SCALE).astype(jnp.bfloat16)
        first = HEADS * NOPE + h * ROPE
        at = slice(h * SPAN, (h + 1) * SPAN)
        for b in range(2 * NX):
            query[b, at, :LAT] = absorbed[b * SPAN : (b + 1) * SPAN]
            part = blocks[b // 2][(b % 2) * SPAN : (b % 2 + 1) * SPAN, first : first + ROPE]
            query[b, at, LAT:] = jnp.concatenate([part, part], axis=1)
    for h in range(HEADS):
        turned_value[h // 2, (h % 2) * VD : (h % 2 + 1) * VD, :] = value_ref[h].T


def in_hbm(value):
    return pltpu.with_memory_space_constraint(value, pltpu.HBM)


def absorb(blocks, key_up, value_up):
    return pl.pallas_call(
        absorb_kernel,
        out_shape=(
            jax.ShapeDtypeStruct((2 * NX, HEADS * SPAN, ROWW), jnp.bfloat16),
            jax.ShapeDtypeStruct((HEADS // 2, 2 * VD, LAT), jnp.bfloat16),
        ),
        in_specs=[HBM] + [WHOLE] * 3 + [HBM] * 2,
        out_specs=(WHOLE, WHOLE),
        scratch_shapes=[
            pltpu.VMEM(blocks[0].shape, jnp.bfloat16),
            pltpu.VMEM(key_up.shape, jnp.bfloat16),
            pltpu.VMEM(value_up.shape, jnp.bfloat16),
            pltpu.SemaphoreType.DMA((3,)),
        ],
        compiler_params=pltpu.CompilerParams(vmem_limit_bytes=VMEM_LIMIT),
    )(in_hbm(blocks[0]), *blocks[1:], in_hbm(key_up), in_hbm(value_up))


def attend_kernel(
    spans_ref, query, own_ref, other_ref, value_ref, out_ref, sorted_keys, latent, contexts, order
):
    zl = lax.axis_index("zl")
    x = lax.axis_index("x")
    c = lax.axis_index("c")

    places = [spans_ref[((i // 2) * NX + x) * 2 + i % 2] for i in range(NSPAN)]

    def earlier(place, among):
        return functools.reduce(jnp.add, [(p < place).astype(jnp.int32) for p in among])

    for i in range(NSPAN):
        rank = earlier(places[i], places)
        for half, keys in enumerate((own_ref, other_ref)):
            for low in range(2):
                target = pl.multiple_of(rank * SPAN + half * 32 + low * 16, 16)
                y = (i % 2) * 2 + low
                first = (i // 2) * NZH * 8
                for j in range(LAT // 128):
                    sorted_keys[pl.ds(target, 16), j * 128 : (j + 1) * 128] = keys[
                        y, j * 128 + first : j * 128 + first + 16, :
                    ]
                tail = keys[y, LAT + first % 64 : LAT + first % 64 + 16, :]
                side = lax.broadcasted_iota(jnp.int32, tail.shape, 1) // ROPE
                sorted_keys[pl.ds(target, 16), LAT:] = jnp.where(side == first // 64, tail, jnp.zeros_like(tail))

    asking = [spans_ref[(zl * NX + (x + NX - b // 2) % NX) * 2 + b % 2] for b in range(2 * NX)]
    for b in range(2 * NX):
        order[earlier(asking[b], asking)] = b

    for n in range(NSPAN * SPAN // CHUNK):
        at = slice(n * CHUNK, (n + 1) * CHUNK)
        latent[:, at] = sorted_keys[at, :LAT].T

    row = lax.broadcasted_iota(jnp.int32, (CHUNK, HEADS * SPAN), 0)
    core = jnp.where(row // 32 % 2 == 0, c, 1 - c)
    key_order = row // SPAN * SPAN + row // 16 % 2 * 32 + row // 8 % 2 * 16 + core * 8 + row % 8
    token = lax.broadcasted_iota(jnp.int32, (1, HEADS * SPAN), 1) % SPAN
    head = lax.broadcasted_iota(jnp.int32, (16, HEADS * SPAN), 1) // SPAN
    dims = (((1,), (1,)), ((), ()))

    def some_spans(turn_of, carry):
        spans = [order[GROUPED * turn_of + i] for i in range(GROUPED)]
        limits = []
        for b in spans:
            source = (x + NX - b // 2) % NX
            below = earlier(spans_ref[(zl * NX + source) * 2 + b % 2], places)
            limits.append(below * SPAN + jnp.where(source == x, token, -1))
            needed = below + (source == x).astype(jnp.int32)
        chunks = jnp.maximum((needed + CHUNK // SPAN - 1) // (CHUNK // SPAN), 1)

        for count in range(1, NSPAN * SPAN // CHUNK + 1):

            @pl.when(chunks == count)
            def _(count=count):
                products = [
                    [
                        lax.dot_general(
                            sorted_keys[n * CHUNK : (n + 1) * CHUNK, :],
                            query[b],
                            dims,
                            preferred_element_type=jnp.float32,
                        )
                        for n in range(count)
                    ]
                    for b in spans
                ]
                for b, limit, scores in zip(spans, limits, products):
                    scores = [
                        jnp.where(key_order <= limit - n * CHUNK, score, LOW) for n, score in enumerate(scores)
                    ]
                    highest = functools.reduce(jnp.maximum, [jnp.max(v, axis=0, keepdims=True) for v in scores])
                    raised = [jnp.exp2(score - highest) for score in scores]
                    total = functools.reduce(jnp.add, [jnp.sum(v, axis=0, keepdims=True) for v in raised])
                    context = jnp.dot(
                        latent[:, : count * CHUNK],
                        jnp.concatenate([v.astype(jnp.bfloat16) for v in raised], axis=0),
                        preferred_element_type=jnp.float32,
                    )
                    contexts[b, :LAT, :] = (context * (1.0 / total)).astype(jnp.bfloat16)
                    log_sum = highest + jnp.log2(total)
                    high = log_sum.astype(jnp.bfloat16).astype(jnp.float32)
                    rest = log_sum - high
                    middle = rest.astype(jnp.bfloat16).astype(jnp.float32)
                    place = lax.broadcasted_iota(jnp.int32, (16, HEADS * SPAN), 0)
                    packed = jnp.where(place < HEADS, high, jnp.where(place < 2 * HEADS, middle, rest - middle))
                    packed = jnp.where((place < 3 * HEADS) & (place % HEADS == head), packed, 0.0)
                    contexts[b, LAT:, :] = packed.astype(jnp.bfloat16)

        return carry

    lax.fori_loop(0, 2 * NX // GROUPED, some_spans, 0)

    left = lax.broadcasted_iota(jnp.int32, (VD, 128), 1) < SPAN
    for p in range(HEADS // 2):
        tile = slice(p * 128, (p + 1) * 128)
        joined = jnp.concatenate([contexts[b, :LAT, tile] for b in range(2 * NX)], axis=1)
        both = jnp.dot(value_ref[p], joined, preferred_element_type=jnp.float32)
        for k in range(NX):
            early, late = [
                jnp.where(left, both[:VD, b * 128 : (b + 1) * 128], both[VD:, b * 128 : (b + 1) * 128])
                for b in (2 * k, 2 * k + 1)
            ]
            target = (x + NX - k) % NX
            for side, values in enumerate(
                (jnp.where(left, early, pltpu.roll(late, SPAN, axis=1)), jnp.where(left, pltpu.roll(early, SPAN, axis=1), late))
            ):
                out_ref[target, (2 * p + side) * VD : (2 * p + side + 1) * VD, :] = values.astype(jnp.bfloat16)
    for k in range(NX):
        logs = []
        for b in (2 * k, 2 * k + 1):
            rows = contexts[b, LAT:, :].astype(jnp.float32)
            rows = rows[:, :128] + rows[:, 128:]
            logs.append(rows + pltpu.roll(rows, SPAN, axis=1))
        out_ref[(x + NX - k) % NX, HEADS * VD :, :] = jnp.where(left[:16], *logs).astype(jnp.bfloat16)


def attend(spans, query, own, other, turned_value):
    return pl.pallas_call(
        attend_kernel,
        out_shape=jax.ShapeDtypeStruct((NX, PARTROWS, 2 * SPAN), jnp.bfloat16),
        in_specs=[SMEM] + [WHOLE] * 4,
        out_specs=WHOLE,
        scratch_shapes=[
            pltpu.VMEM((NSPAN * SPAN, ROWW), jnp.bfloat16),
            pltpu.VMEM((LAT, NSPAN * SPAN), jnp.bfloat16),
            pltpu.VMEM((2 * NX, LAT + 16, HEADS * SPAN), jnp.bfloat16),
            pltpu.SMEM((2 * NX,), jnp.int32),
        ],
        compiler_params=pltpu.CompilerParams(vmem_limit_bytes=VMEM_LIMIT),
    )(spans, query, own, other, turned_value)


def replicate_kernel(keys_ref, out_ref):
    rows = keys_ref.shape[0]
    side = lax.broadcasted_iota(jnp.int32, (rows // 2, 128), 1) < ROPE
    tail = jnp.where(side, keys_ref[: rows // 2, LAT:], keys_ref[rows // 2 :, LAT:])
    for k in range(NY):
        for j in range(LAT // 128):
            out_ref[k, j * rows : (j + 1) * rows, :] = keys_ref[:, j * 128 : (j + 1) * 128]
        out_ref[k, LAT // 128 * rows :, :] = tail


def replicate(keys):
    return pl.pallas_call(
        replicate_kernel,
        out_shape=jax.ShapeDtypeStruct((NY, keys.shape[0] * KEYW // 128, 128), jnp.bfloat16),
        in_specs=[WHOLE],
        out_specs=WHOLE,
        compiler_params=pltpu.CompilerParams(vmem_limit_bytes=VMEM_LIMIT),
    )(keys)


def add_kernel(first_ref, second_ref, out_ref):
    out_ref[...] = (first_ref[...].astype(jnp.float32) + second_ref[...].astype(jnp.float32)).astype(jnp.bfloat16)


def added(first, second):
    return pl.pallas_call(
        add_kernel,
        out_shape=jax.ShapeDtypeStruct(first.shape, jnp.bfloat16),
        in_specs=[WHOLE, WHOLE],
        out_specs=WHOLE,
        compiler_params=pltpu.CompilerParams(vmem_limit_bytes=VMEM_LIMIT),
    )(first, second)


def project_kernel(parts_ref, weight_ref, send_ref, keep_ref):
    c = lax.axis_index("c")
    heads = []
    packed = [parts_ref[i, HEADS * VD :, :].astype(jnp.float32) for i in range(NX)]
    for h in range(HEADS):
        logs = [(p[h : h + 1] + p[HEADS + h : HEADS + h + 1]) + p[2 * HEADS + h : 2 * HEADS + h + 1] for p in packed]
        highest = functools.reduce(jnp.maximum, logs)
        shares = [jnp.exp2(v - highest) for v in logs]
        inverse = 1.0 / functools.reduce(jnp.add, shares)
        merged = functools.reduce(
            jnp.add,
            [
                (shares[i] * inverse) * parts_ref[i, h * VD : (h + 1) * VD, :].astype(jnp.float32)
                for i in range(NX)
            ],
        )
        heads.append(merged.T.astype(jnp.bfloat16))
    head_out = jnp.concatenate(heads, axis=1)
    step = weight_ref.shape[1] // NY
    width = step // (NZH * NC)
    for y in range(NY):
        result = jnp.dot(
            head_out, weight_ref[:, y * step : (y + 1) * step], preferred_element_type=jnp.float32
        ).T.astype(jnp.bfloat16)
        for zh in range(NZH):
            even = result[2 * zh * width : (2 * zh + 1) * width]
            odd = result[(2 * zh + 1) * width : (2 * zh + 2) * width]
            keep_ref[y, zh] = jnp.where(c == 0, even, odd)
            send_ref[y, zh] = jnp.where(c == 0, odd, even)


def project(parts, weight):
    width = weight.shape[1] // (NY * NZH * NC)
    piece = jax.ShapeDtypeStruct((NY, NZH, width, 2 * SPAN), jnp.bfloat16)
    return pl.pallas_call(
        project_kernel,
        out_shape=(piece, piece),
        in_specs=[WHOLE, WHOLE],
        out_specs=(WHOLE, WHOLE),
        compiler_params=pltpu.CompilerParams(vmem_limit_bytes=VMEM_LIMIT),
    )(parts, weight)


def shifted(value, by):
    return lax.ppermute(value, "x", [(i, (i + by) % NX) for i in range(NX)])


def swapped(value, axis):
    return lax.ppermute(value, axis, [(0, 1), (1, 0)])


def exchanged(value, axis):
    return lax.all_to_all(value, axis, split_axis=0, concat_axis=0, tiled=True)


def on_device(query_plain, query_rotary, latent_keys, span_order, key_up, value_up, output_weight):
    zh = lax.axis_index("zh")
    tables = jnp.asarray(rotary_tables())
    sent_keys = pl.pallas_call(
        keys_kernel,
        out_shape=jax.ShapeDtypeStruct((GROUP, 8, ROWW), jnp.bfloat16),
        in_specs=[SMEM, WHOLE, WHOLE],
        out_specs=WHOLE,
    )(span_order, latent_keys, tables)
    rows = jax.ShapeDtypeStruct((2 * SPAN, QW), jnp.bfloat16)
    queries, kept_spans = pl.pallas_call(
        queries_kernel,
        out_shape=(rows, jax.ShapeDtypeStruct(span_order.shape, span_order.dtype)),
        in_specs=[SMEM, WHOLE, WHOLE, WHOLE, pl.BlockSpec(memory_space=pl.ANY)],
        out_specs=(WHOLE, SMEM),
    )(span_order, query_plain, query_rotary, tables, sent_keys)
    along_z = exchanged(sent_keys, ("zl", "zh")).reshape(GROUP * 8, ROWW)
    blocks = [queries, shifted(queries, 1), None, shifted(queries, NX - 1)]
    along_z, blocks[1], blocks[3] = lax.optimization_barrier((along_z, blocks[1], blocks[3]))
    blocks[2] = shifted(blocks[1], 1)
    own = exchanged(replicate(along_z), "y")
    own, blocks[2] = lax.optimization_barrier((own, blocks[2]))
    other = swapped(own, "c")
    query, turned_value = absorb(blocks, key_up, value_up)
    parts = attend(kept_spans, query, own, other, turned_value)
    send, keep = project(exchanged(parts, "x"), output_weight)
    both = added(keep, swapped(send, "c"))
    over_y = exchanged(both, "y").astype(jnp.float32)
    mine = jnp.sum(lax.dynamic_index_in_dim(over_y, zh, 1, keepdims=False), axis=0)
    theirs = jnp.sum(lax.dynamic_index_in_dim(over_y, 1 - zh, 1, keepdims=False), axis=0).astype(jnp.bfloat16)
    return (mine + swapped(theirs, "zh").astype(jnp.float32)).astype(jnp.bfloat16).T


def solution(mesh):
    finer = Mesh(
        mesh.devices.reshape(NZL, NX, NY, NZH, NC), ("zl", "x", "y", "zh", "c")
    )
    in_specs = (
        P(CTX, TP),
        P(CTX, TP),
        P(CTX + TP, None),
        P(),
        P(TP, None, None),
        P(TP, None, None),
        P(TP, None),
    )
    return jax.shard_map(
        on_device, mesh=finer, in_specs=in_specs, out_specs=P(CTX, TP), check_vma=False
    )
```

```python
import functools
import math

import jax
import jax.numpy as jnp
import numpy as np
from jax import lax
from jax.experimental import pallas as pl
from jax.experimental.pallas import tpu as pltpu
from jax.sharding import Mesh
from jax.sharding import PartitionSpec as P

NZL, NX, NY, NZH, NC = 8, 4, 4, 2, 2
CTX = ("zl", "x")
TP = ("y", "zh", "c")

SPAN = 64
ROPE = 64
LAT = 512
NOPE = 128
VD = 128
HEADS = 4
KEYW = LAT + ROPE
ROWW = 640
GROUP = NZL * NZH
NSPAN = 2 * NZL
CHUNK = 256
GROUPED = 4
QW = HEADS * (NOPE + ROPE)
PARTROWS = HEADS * VD + 16
BASE = 10000.0
LOW = -1e30
SCALE = math.log2(math.e) / math.sqrt(NOPE + ROPE)
MIB = 1024 * 1024


def rotary_tables():
    lane = np.arange(128)
    freq = BASE ** (-2.0 * (lane % 32) / ROPE)
    sign = np.where(lane % 64 < 32, -1.0, 1.0)
    start = (np.arange(64) * SPAN)[:, None] * freq[None, :]
    offset = np.arange(SPAN)[:, None] * freq[None, :]
    tables = [np.cos(start), sign * np.sin(start), np.cos(offset), sign * np.sin(offset)]
    return np.stack(tables).astype(np.float32)


def turn(values, cosine, signed_sine):
    lane = lax.broadcasted_iota(jnp.int32, values.shape, 1)
    partner = jnp.where(
        lane % 64 < 32, pltpu.roll(values, 96, axis=1), pltpu.roll(values, 32, axis=1)
    )
    return values * cosine + partner * signed_sine


def angle_of(tables_ref, span, offset_rows):
    cos_a = tables_ref[0, pl.ds(span, 1), :]
    sin_a = tables_ref[1, pl.ds(span, 1), :]
    cos_b = tables_ref[2, offset_rows, :]
    sin_b = tables_ref[3, offset_rows, :]
    return cos_a * cos_b - sin_a * sin_b, sin_a * cos_b + cos_a * sin_b


def own_ctx():
    return lax.axis_index("zl") * NX + lax.axis_index("x")


def own_tp():
    return (lax.axis_index("y") * NZH + lax.axis_index("zh")) * NC + lax.axis_index("c")


def keys_kernel(spans_ref, keys_ref, tables_ref, out_ref):
    tp = own_tp()
    span = spans_ref[own_ctx() * 2 + tp // 8]
    first = pl.multiple_of((tp % 8) * 8, 8)
    cosine, sine = angle_of(tables_ref, span, pl.ds(first, 8))
    tail = keys_ref[:, LAT:].astype(jnp.float32)
    turned = turn(jnp.concatenate([tail, tail], axis=1), cosine, sine).astype(jnp.bfloat16)
    for k in range(GROUP):
        out_ref[k, :, :LAT] = keys_ref[:, :LAT]
        out_ref[k, :, LAT:] = turned


def queries_kernel(spans_ref, plain_ref, rotary_ref, tables_ref, after_ref, out_ref, kept_spans_ref):
    out_ref[:, : HEADS * NOPE] = plain_ref[...]
    for s in range(2):
        rows = slice(s * SPAN, (s + 1) * SPAN)
        cosine, sine = angle_of(tables_ref, spans_ref[own_ctx() * 2 + s], pl.ds(0, SPAN))
        for j in range(HEADS * ROPE // 128):
            part = rotary_ref[rows, j * 128 : (j + 1) * 128].astype(jnp.float32)
            at = HEADS * NOPE + j * 128
            out_ref[rows, at : at + 128] = (turn(part, cosine, sine) * SCALE).astype(jnp.bfloat16)
    for i in range(kept_spans_ref.shape[0]):
        kept_spans_ref[i] = spans_ref[i]


SMEM = pl.BlockSpec(memory_space=pltpu.SMEM)
WHOLE = pl.BlockSpec(memory_space=pltpu.VMEM)
HBM = pl.BlockSpec(memory_space=pltpu.HBM)


def absorb_kernel(*refs):
    sources, (query, turned_value), targets, arrived = refs[:6], refs[6:8], refs[8:14], refs[14]
    q0, q1, q2, q3, up_ref, value_ref = targets
    fetches = [
        pltpu.make_async_copy(source, target, arrived.at[i])
        for i, (source, target) in enumerate(zip(sources, targets))
    ]
    for fetch in fetches:
        fetch.start()
    for fetch in fetches:
        fetch.wait()
    blocks = (q0, q1, q2, q3)
    for h in range(HEADS):
        plain = jnp.concatenate([block[:, h * NOPE : (h + 1) * NOPE] for block in blocks], axis=0)
        absorbed = (jnp.dot(plain, up_ref[h], preferred_element_type=jnp.float32) * SCALE).astype(jnp.bfloat16)
        first = HEADS * NOPE + h * ROPE
        at = slice(h * SPAN, (h + 1) * SPAN)
        for b in range(2 * NX):
            query[b, at, :LAT] = absorbed[b * SPAN : (b + 1) * SPAN]
            part = blocks[b // 2][(b % 2) * SPAN : (b % 2 + 1) * SPAN, first : first + ROPE]
            query[b, at, LAT:] = jnp.concatenate([part, part], axis=1)
    for h in range(HEADS):
        turned_value[h // 2, (h % 2) * VD : (h % 2 + 1) * VD, :] = value_ref[h].T


def in_hbm(value):
    return pltpu.with_memory_space_constraint(value, pltpu.HBM)


def absorb(blocks, key_up, value_up):
    return pl.pallas_call(
        absorb_kernel,
        out_shape=(
            jax.ShapeDtypeStruct((2 * NX, HEADS * SPAN, ROWW), jnp.bfloat16),
            jax.ShapeDtypeStruct((HEADS // 2, 2 * VD, LAT), jnp.bfloat16),
        ),
        in_specs=[HBM] * 6,
        out_specs=(WHOLE, WHOLE),
        scratch_shapes=[
            *[pltpu.VMEM(v.shape, jnp.bfloat16) for v in (*blocks, key_up, value_up)],
            pltpu.SemaphoreType.DMA((6,)),
        ],
        compiler_params=pltpu.CompilerParams(vmem_limit_bytes=16 * MIB),
    )(*[in_hbm(v) for v in (*blocks, key_up, value_up)])


def attend_kernel(
    spans_ref, query, own_ref, other_ref, value_hbm, out_ref, sorted_keys, latent, contexts, order, value_ref, arrived
):
    fetch = pltpu.make_async_copy(value_hbm, value_ref, arrived)
    fetch.start()
    zl = lax.axis_index("zl")
    x = lax.axis_index("x")
    c = lax.axis_index("c")

    places = [spans_ref[((i // 2) * NX + x) * 2 + i % 2] for i in range(NSPAN)]

    def earlier(place, among):
        return functools.reduce(jnp.add, [(p < place).astype(jnp.int32) for p in among])

    for i in range(NSPAN):
        rank = earlier(places[i], places)
        for half, keys in enumerate((own_ref, other_ref)):
            for low in range(2):
                target = pl.multiple_of(rank * SPAN + half * 32 + low * 16, 16)
                y = (i % 2) * 2 + low
                first = (i // 2) * NZH * 8
                for j in range(LAT // 128):
                    sorted_keys[pl.ds(target, 16), j * 128 : (j + 1) * 128] = keys[
                        y, j * 128 + first : j * 128 + first + 16, :
                    ]
                tail = keys[y, LAT + first % 64 : LAT + first % 64 + 16, :]
                side = lax.broadcasted_iota(jnp.int32, tail.shape, 1) // ROPE
                sorted_keys[pl.ds(target, 16), LAT:] = jnp.where(side == first // 64, tail, jnp.zeros_like(tail))

    asking = [spans_ref[(zl * NX + (x + NX - b // 2) % NX) * 2 + b % 2] for b in range(2 * NX)]
    for b in range(2 * NX):
        order[earlier(asking[b], asking)] = b

    for n in range(NSPAN * SPAN // CHUNK):
        at = slice(n * CHUNK, (n + 1) * CHUNK)
        latent[:, at] = sorted_keys[at, :LAT].T

    row = lax.broadcasted_iota(jnp.int32, (CHUNK, HEADS * SPAN), 0)
    core = jnp.where(row // 32 % 2 == 0, c, 1 - c)
    key_order = row // SPAN * SPAN + row // 16 % 2 * 32 + row // 8 % 2 * 16 + core * 8 + row % 8
    token = lax.broadcasted_iota(jnp.int32, (1, HEADS * SPAN), 1) % SPAN
    head = lax.broadcasted_iota(jnp.int32, (16, HEADS * SPAN), 1) // SPAN
    dims = (((1,), (1,)), ((), ()))

    def some_spans(turn_of, carry):
        spans = [order[GROUPED * turn_of + i] for i in range(GROUPED)]
        limits = []
        for b in spans:
            source = (x + NX - b // 2) % NX
            below = earlier(spans_ref[(zl * NX + source) * 2 + b % 2], places)
            limits.append(below * SPAN + jnp.where(source == x, token, -1))
            needed = below + (source == x).astype(jnp.int32)
        chunks = jnp.maximum((needed + CHUNK // SPAN - 1) // (CHUNK // SPAN), 1)

        for count in range(1, NSPAN * SPAN // CHUNK + 1):

            @pl.when(chunks == count)
            def _(count=count):
                products = [
                    [
                        lax.dot_general(
                            sorted_keys[n * CHUNK : (n + 1) * CHUNK, :],
                            query[b],
                            dims,
                            preferred_element_type=jnp.float32,
                        )
                        for n in range(count)
                    ]
                    for b in spans
                ]
                for b, limit, scores in zip(spans, limits, products):
                    scores = [
                        jnp.where(key_order <= limit - n * CHUNK, score, LOW) for n, score in enumerate(scores)
                    ]
                    highest = functools.reduce(jnp.maximum, [jnp.max(v, axis=0, keepdims=True) for v in scores])
                    raised = [jnp.exp2(score - highest) for score in scores]
                    total = functools.reduce(jnp.add, [jnp.sum(v, axis=0, keepdims=True) for v in raised])
                    context = jnp.dot(
                        latent[:, : count * CHUNK],
                        jnp.concatenate([v.astype(jnp.bfloat16) for v in raised], axis=0),
                        preferred_element_type=jnp.float32,
                    )
                    contexts[b, :LAT, :] = (context * (1.0 / total)).astype(jnp.bfloat16)
                    log_sum = highest + jnp.log2(total)
                    high = log_sum.astype(jnp.bfloat16).astype(jnp.float32)
                    rest = log_sum - high
                    middle = rest.astype(jnp.bfloat16).astype(jnp.float32)
                    place = lax.broadcasted_iota(jnp.int32, (16, HEADS * SPAN), 0)
                    packed = jnp.where(place < HEADS, high, jnp.where(place < 2 * HEADS, middle, rest - middle))
                    packed = jnp.where((place < 3 * HEADS) & (place % HEADS == head), packed, 0.0)
                    contexts[b, LAT:, :] = packed.astype(jnp.bfloat16)

        return carry

    lax.fori_loop(0, 2 * NX // GROUPED, some_spans, 0)

    fetch.wait()
    left = lax.broadcasted_iota(jnp.int32, (VD, 128), 1) < SPAN
    for p in range(HEADS // 2):
        tile = slice(p * 128, (p + 1) * 128)
        joined = jnp.concatenate([contexts[b, :LAT, tile] for b in range(2 * NX)], axis=1)
        both = jnp.dot(value_ref[p], joined, preferred_element_type=jnp.float32)
        for k in range(NX):
            early, late = [
                jnp.where(left, both[:VD, b * 128 : (b + 1) * 128], both[VD:, b * 128 : (b + 1) * 128])
                for b in (2 * k, 2 * k + 1)
            ]
            target = (x + NX - k) % NX
            for side, values in enumerate(
                (jnp.where(left, early, pltpu.roll(late, SPAN, axis=1)), jnp.where(left, pltpu.roll(early, SPAN, axis=1), late))
            ):
                out_ref[target, (2 * p + side) * VD : (2 * p + side + 1) * VD, :] = values.astype(jnp.bfloat16)
    for k in range(NX):
        logs = []
        for b in (2 * k, 2 * k + 1):
            rows = contexts[b, LAT:, :].astype(jnp.float32)
            rows = rows[:, :128] + rows[:, 128:]
            logs.append(rows + pltpu.roll(rows, SPAN, axis=1))
        out_ref[(x + NX - k) % NX, HEADS * VD :, :] = jnp.where(left[:16], *logs).astype(jnp.bfloat16)


def attend(spans, query, own, other, turned_value):
    return pl.pallas_call(
        attend_kernel,
        out_shape=jax.ShapeDtypeStruct((NX, PARTROWS, 2 * SPAN), jnp.bfloat16),
        in_specs=[SMEM] + [WHOLE] * 3 + [HBM],
        out_specs=WHOLE,
        scratch_shapes=[
            pltpu.VMEM((NSPAN * SPAN, ROWW), jnp.bfloat16),
            pltpu.VMEM((LAT, NSPAN * SPAN), jnp.bfloat16),
            pltpu.VMEM((2 * NX, LAT + 16, HEADS * SPAN), jnp.bfloat16),
            pltpu.SMEM((2 * NX,), jnp.int32),
            pltpu.VMEM(turned_value.shape, jnp.bfloat16),
            pltpu.SemaphoreType.DMA(()),
        ],
        compiler_params=pltpu.CompilerParams(vmem_limit_bytes=28 * MIB),
    )(spans, query, own, other, in_hbm(turned_value))


def replicate_kernel(keys_ref, out_ref):
    rows = keys_ref.shape[0]
    side = lax.broadcasted_iota(jnp.int32, (rows // 2, 128), 1) < ROPE
    tail = jnp.where(side, keys_ref[: rows // 2, LAT:], keys_ref[rows // 2 :, LAT:])
    for k in range(NY):
        for j in range(LAT // 128):
            out_ref[k, j * rows : (j + 1) * rows, :] = keys_ref[:, j * 128 : (j + 1) * 128]
        out_ref[k, LAT // 128 * rows :, :] = tail


def replicate(keys):
    return pl.pallas_call(
        replicate_kernel,
        out_shape=jax.ShapeDtypeStruct((NY, keys.shape[0] * KEYW // 128, 128), jnp.bfloat16),
        in_specs=[WHOLE],
        out_specs=WHOLE,
        compiler_params=pltpu.CompilerParams(vmem_limit_bytes=6 * MIB),
    )(keys)


def add_kernel(first_ref, second_ref, out_ref):
    out_ref[...] = (first_ref[...].astype(jnp.float32) + second_ref[...].astype(jnp.float32)).astype(jnp.bfloat16)


def added(first, second):
    return pl.pallas_call(
        add_kernel,
        out_shape=jax.ShapeDtypeStruct(first.shape, jnp.bfloat16),
        in_specs=[WHOLE, WHOLE],
        out_specs=WHOLE,
        compiler_params=pltpu.CompilerParams(vmem_limit_bytes=6 * MIB),
    )(first, second)


def project_kernel(parts_ref, weight_ref, send_ref, keep_ref):
    c = lax.axis_index("c")
    heads = []
    packed = [parts_ref[i, HEADS * VD :, :].astype(jnp.float32) for i in range(NX)]
    for h in range(HEADS):
        logs = [(p[h : h + 1] + p[HEADS + h : HEADS + h + 1]) + p[2 * HEADS + h : 2 * HEADS + h + 1] for p in packed]
        highest = functools.reduce(jnp.maximum, logs)
        shares = [jnp.exp2(v - highest) for v in logs]
        inverse = 1.0 / functools.reduce(jnp.add, shares)
        merged = functools.reduce(
            jnp.add,
            [
                (shares[i] * inverse) * parts_ref[i, h * VD : (h + 1) * VD, :].astype(jnp.float32)
                for i in range(NX)
            ],
        )
        heads.append(merged.T.astype(jnp.bfloat16))
    head_out = jnp.concatenate(heads, axis=1)
    step = weight_ref.shape[1] // NY
    width = step // (NZH * NC)
    for y in range(NY):
        result = jnp.dot(
            head_out, weight_ref[:, y * step : (y + 1) * step], preferred_element_type=jnp.float32
        ).T.astype(jnp.bfloat16)
        for zh in range(NZH):
            even = result[2 * zh * width : (2 * zh + 1) * width]
            odd = result[(2 * zh + 1) * width : (2 * zh + 2) * width]
            keep_ref[y, zh] = jnp.where(c == 0, even, odd)
            send_ref[y, zh] = jnp.where(c == 0, odd, even)


def project(parts, weight):
    width = weight.shape[1] // (NY * NZH * NC)
    piece = jax.ShapeDtypeStruct((NY, NZH, width, 2 * SPAN), jnp.bfloat16)
    return pl.pallas_call(
        project_kernel,
        out_shape=(piece, piece),
        in_specs=[WHOLE, WHOLE],
        out_specs=(WHOLE, WHOLE),
        compiler_params=pltpu.CompilerParams(vmem_limit_bytes=20 * MIB),
    )(parts, weight)


def shifted(value, by):
    return lax.ppermute(value, "x", [(i, (i + by) % NX) for i in range(NX)])


def swapped(value, axis):
    return lax.ppermute(value, axis, [(0, 1), (1, 0)])


def exchanged(value, axis):
    return lax.all_to_all(value, axis, split_axis=0, concat_axis=0, tiled=True)


def on_device(query_plain, query_rotary, latent_keys, span_order, key_up, value_up, output_weight):
    zh = lax.axis_index("zh")
    tables = jnp.asarray(rotary_tables())
    sent_keys = pl.pallas_call(
        keys_kernel,
        out_shape=jax.ShapeDtypeStruct((GROUP, 8, ROWW), jnp.bfloat16),
        in_specs=[SMEM, WHOLE, WHOLE],
        out_specs=WHOLE,
    )(span_order, latent_keys, tables)
    rows = jax.ShapeDtypeStruct((2 * SPAN, QW), jnp.bfloat16)
    queries, kept_spans = pl.pallas_call(
        queries_kernel,
        out_shape=(rows, jax.ShapeDtypeStruct(span_order.shape, span_order.dtype)),
        in_specs=[SMEM, WHOLE, WHOLE, WHOLE, pl.BlockSpec(memory_space=pl.ANY)],
        out_specs=(WHOLE, SMEM),
    )(span_order, query_plain, query_rotary, tables, sent_keys)
    along_z = exchanged(sent_keys, ("zl", "zh")).reshape(GROUP * 8, ROWW)
    blocks = [queries, shifted(queries, 1), None, shifted(queries, NX - 1)]
    blocks[2] = shifted(blocks[1], 1)
    along_z, *blocks = lax.optimization_barrier((along_z, *blocks))
    query, turned_value = absorb(blocks, key_up, value_up)
    own = exchanged(replicate(along_z), "y")
    own, query, turned_value = lax.optimization_barrier((own, query, turned_value))
    other = swapped(own, "c")
    parts = attend(kept_spans, query, own, other, turned_value)
    send, keep = project(exchanged(parts, "x"), output_weight)
    both = added(keep, swapped(send, "c"))
    over_y = exchanged(both, "y").astype(jnp.float32)
    mine = jnp.sum(lax.dynamic_index_in_dim(over_y, zh, 1, keepdims=False), axis=0)
    theirs = jnp.sum(lax.dynamic_index_in_dim(over_y, 1 - zh, 1, keepdims=False), axis=0).astype(jnp.bfloat16)
    return (mine + swapped(theirs, "zh").astype(jnp.float32)).astype(jnp.bfloat16).T


def solution(mesh):
    finer = Mesh(
        mesh.devices.reshape(NZL, NX, NY, NZH, NC), ("zl", "x", "y", "zh", "c")
    )
    in_specs = (
        P(CTX, TP),
        P(CTX, TP),
        P(CTX + TP, None),
        P(),
        P(TP, None, None),
        P(TP, None, None),
        P(TP, None),
    )
    return jax.shard_map(
        on_device, mesh=finer, in_specs=in_specs, out_specs=P(CTX, TP), check_vma=False
    )
```

```python
import functools
import math

import jax
import jax.numpy as jnp
import numpy as np
from jax import lax
from jax.experimental import pallas as pl
from jax.experimental.pallas import tpu as pltpu
from jax.sharding import Mesh
from jax.sharding import PartitionSpec as P

NZL, NX, NY, NZH, NC = 8, 4, 4, 2, 2
CTX = ("zl", "x")
TP = ("y", "zh", "c")

SPAN = 64
ROPE = 64
LAT = 512
NOPE = 128
VD = 128
HEADS = 4
KEYW = LAT + ROPE
ROWW = 640
GROUP = NZL * NZH
NSPAN = 2 * NZL
CHUNK = 256
GROUPED = 4
QW = HEADS * (NOPE + ROPE)
PARTROWS = HEADS * VD + 16
BASE = 10000.0
LOW = -1e30
SCALE = math.log2(math.e) / math.sqrt(NOPE + ROPE)
VMEM_LIMIT = 48 * 1024 * 1024


def rotary_tables():
    lane = np.arange(128)
    freq = BASE ** (-2.0 * (lane % 32) / ROPE)
    sign = np.where(lane % 64 < 32, -1.0, 1.0)
    start = (np.arange(64) * SPAN)[:, None] * freq[None, :]
    offset = np.arange(SPAN)[:, None] * freq[None, :]
    tables = [np.cos(start), sign * np.sin(start), np.cos(offset), sign * np.sin(offset)]
    return np.stack(tables).astype(np.float32)


def turn(values, cosine, signed_sine):
    lane = lax.broadcasted_iota(jnp.int32, values.shape, 1)
    partner = jnp.where(
        lane % 64 < 32, pltpu.roll(values, 96, axis=1), pltpu.roll(values, 32, axis=1)
    )
    return values * cosine + partner * signed_sine


def angle_of(tables_ref, span, offset_rows):
    cos_a = tables_ref[0, pl.ds(span, 1), :]
    sin_a = tables_ref[1, pl.ds(span, 1), :]
    cos_b = tables_ref[2, offset_rows, :]
    sin_b = tables_ref[3, offset_rows, :]
    return cos_a * cos_b - sin_a * sin_b, sin_a * cos_b + cos_a * sin_b


def own_ctx():
    return lax.axis_index("zl") * NX + lax.axis_index("x")


def own_tp():
    return (lax.axis_index("y") * NZH + lax.axis_index("zh")) * NC + lax.axis_index("c")


def keys_kernel(spans_ref, keys_ref, tables_ref, out_ref):
    tp = own_tp()
    span = spans_ref[own_ctx() * 2 + tp // 8]
    first = pl.multiple_of((tp % 8) * 8, 8)
    cosine, sine = angle_of(tables_ref, span, pl.ds(first, 8))
    tail = keys_ref[:, LAT:].astype(jnp.float32)
    turned = turn(jnp.concatenate([tail, tail], axis=1), cosine, sine).astype(jnp.bfloat16)
    for k in range(GROUP):
        out_ref[k, :, :LAT] = keys_ref[:, :LAT]
        out_ref[k, :, LAT:] = turned


def queries_kernel(spans_ref, plain_ref, rotary_ref, tables_ref, after_ref, out_ref, kept_spans_ref):
    out_ref[:, : HEADS * NOPE] = plain_ref[...]
    for s in range(2):
        rows = slice(s * SPAN, (s + 1) * SPAN)
        cosine, sine = angle_of(tables_ref, spans_ref[own_ctx() * 2 + s], pl.ds(0, SPAN))
        for j in range(HEADS * ROPE // 128):
            part = rotary_ref[rows, j * 128 : (j + 1) * 128].astype(jnp.float32)
            at = HEADS * NOPE + j * 128
            out_ref[rows, at : at + 128] = (turn(part, cosine, sine) * SCALE).astype(jnp.bfloat16)
    for i in range(kept_spans_ref.shape[0]):
        kept_spans_ref[i] = spans_ref[i]


SMEM = pl.BlockSpec(memory_space=pltpu.SMEM)
WHOLE = pl.BlockSpec(memory_space=pltpu.VMEM)
HBM = pl.BlockSpec(memory_space=pltpu.HBM)


def absorb_kernel(q0_hbm, q1, q2, q3, up_hbm, value_hbm, query, turned_value, q0, up_ref, value_ref, arrived):
    fetches = [
        pltpu.make_async_copy(source, target, arrived.at[i])
        for i, (source, target) in enumerate(((q0_hbm, q0), (up_hbm, up_ref), (value_hbm, value_ref)))
    ]
    for fetch in fetches:
        fetch.start()
    for fetch in fetches:
        fetch.wait()
    blocks = (q0, q1, q2, q3)
    for h in range(HEADS):
        plain = jnp.concatenate([block[:, h * NOPE : (h + 1) * NOPE] for block in blocks], axis=0)
        absorbed = (jnp.dot(plain, up_ref[h], preferred_element_type=jnp.float32) * SCALE).astype(jnp.bfloat16)
        first = HEADS * NOPE + h * ROPE
        at = slice(h * SPAN, (h + 1) * SPAN)
        for b in range(2 * NX):
            query[b, at, :LAT] = absorbed[b * SPAN : (b + 1) * SPAN]
            part = blocks[b // 2][(b % 2) * SPAN : (b % 2 + 1) * SPAN, first : first + ROPE]
            query[b, at, LAT:] = jnp.concatenate([part, part], axis=1)
    for h in range(HEADS):
        turned_value[h // 2, (h % 2) * VD : (h % 2 + 1) * VD, :] = value_ref[h].T


def in_hbm(value):
    return pltpu.with_memory_space_constraint(value, pltpu.HBM)


def absorb(blocks, key_up, value_up):
    return pl.pallas_call(
        absorb_kernel,
        out_shape=(
            jax.ShapeDtypeStruct((2 * NX, HEADS * SPAN, ROWW), jnp.bfloat16),
            jax.ShapeDtypeStruct((HEADS // 2, 2 * VD, LAT), jnp.bfloat16),
        ),
        in_specs=[HBM] + [WHOLE] * 3 + [HBM] * 2,
        out_specs=(WHOLE, WHOLE),
        scratch_shapes=[
            pltpu.VMEM(blocks[0].shape, jnp.bfloat16),
            pltpu.VMEM(key_up.shape, jnp.bfloat16),
            pltpu.VMEM(value_up.shape, jnp.bfloat16),
            pltpu.SemaphoreType.DMA((3,)),
        ],
        compiler_params=pltpu.CompilerParams(vmem_limit_bytes=VMEM_LIMIT),
    )(in_hbm(blocks[0]), *blocks[1:], in_hbm(key_up), in_hbm(value_up))


def attend_kernel(
    spans_ref, query, own_ref, other_ref, value_ref, out_ref, sorted_keys, latent, contexts, order
):
    zl = lax.axis_index("zl")
    x = lax.axis_index("x")
    c = lax.axis_index("c")

    places = [spans_ref[((i // 2) * NX + x) * 2 + i % 2] for i in range(NSPAN)]

    def earlier(place, among):
        return functools.reduce(jnp.add, [(p < place).astype(jnp.int32) for p in among])

    for i in range(NSPAN):
        rank = earlier(places[i], places)
        for half, keys in enumerate((own_ref, other_ref)):
            for low in range(2):
                target = pl.multiple_of(rank * SPAN + half * 32 + low * 16, 16)
                y = (i % 2) * 2 + low
                first = (i // 2) * NZH * 8
                for j in range(LAT // 128):
                    sorted_keys[pl.ds(target, 16), j * 128 : (j + 1) * 128] = keys[
                        y, j * 128 + first : j * 128 + first + 16, :
                    ]
                tail = keys[y, LAT + first % 64 : LAT + first % 64 + 16, :]
                side = lax.broadcasted_iota(jnp.int32, tail.shape, 1) // ROPE
                sorted_keys[pl.ds(target, 16), LAT:] = jnp.where(side == first // 64, tail, jnp.zeros_like(tail))

    asking = [spans_ref[(zl * NX + (x + NX - b // 2) % NX) * 2 + b % 2] for b in range(2 * NX)]
    for b in range(2 * NX):
        order[earlier(asking[b], asking)] = b

    for n in range(NSPAN * SPAN // CHUNK):
        at = slice(n * CHUNK, (n + 1) * CHUNK)
        latent[:, at] = sorted_keys[at, :LAT].T

    row = lax.broadcasted_iota(jnp.int32, (CHUNK, HEADS * SPAN), 0)
    core = jnp.where(row // 32 % 2 == 0, c, 1 - c)
    key_order = row // SPAN * SPAN + row // 16 % 2 * 32 + row // 8 % 2 * 16 + core * 8 + row % 8
    token = lax.broadcasted_iota(jnp.int32, (1, HEADS * SPAN), 1) % SPAN
    head = lax.broadcasted_iota(jnp.int32, (16, HEADS * SPAN), 1) // SPAN
    dims = (((1,), (1,)), ((), ()))

    def some_spans(turn_of, carry):
        spans = [order[GROUPED * turn_of + i] for i in range(GROUPED)]
        limits = []
        for b in spans:
            source = (x + NX - b // 2) % NX
            below = earlier(spans_ref[(zl * NX + source) * 2 + b % 2], places)
            limits.append(below * SPAN + jnp.where(source == x, token, -1))
            needed = below + (source == x).astype(jnp.int32)
        chunks = jnp.maximum((needed + CHUNK // SPAN - 1) // (CHUNK // SPAN), 1)

        for count in range(1, NSPAN * SPAN // CHUNK + 1):

            @pl.when(chunks == count)
            def _(count=count):
                products = [
                    [
                        lax.dot_general(
                            sorted_keys[n * CHUNK : (n + 1) * CHUNK, :],
                            query[b],
                            dims,
                            preferred_element_type=jnp.float32,
                        )
                        for n in range(count)
                    ]
                    for b in spans
                ]
                for b, limit, scores in zip(spans, limits, products):
                    scores = [
                        jnp.where(key_order <= limit - n * CHUNK, score, LOW) for n, score in enumerate(scores)
                    ]
                    highest = functools.reduce(jnp.maximum, [jnp.max(v, axis=0, keepdims=True) for v in scores])
                    raised = [jnp.exp2(score - highest) for score in scores]
                    total = functools.reduce(jnp.add, [jnp.sum(v, axis=0, keepdims=True) for v in raised])
                    context = jnp.dot(
                        latent[:, : count * CHUNK],
                        jnp.concatenate([v.astype(jnp.bfloat16) for v in raised], axis=0),
                        preferred_element_type=jnp.float32,
                    )
                    contexts[b, :LAT, :] = (context * (1.0 / total)).astype(jnp.bfloat16)
                    log_sum = highest + jnp.log2(total)
                    high = log_sum.astype(jnp.bfloat16).astype(jnp.float32)
                    rest = log_sum - high
                    middle = rest.astype(jnp.bfloat16).astype(jnp.float32)
                    place = lax.broadcasted_iota(jnp.int32, (16, HEADS * SPAN), 0)
                    packed = jnp.where(place < HEADS, high, jnp.where(place < 2 * HEADS, middle, rest - middle))
                    packed = jnp.where((place < 3 * HEADS) & (place % HEADS == head), packed, 0.0)
                    contexts[b, LAT:, :] = packed.astype(jnp.bfloat16)

        return carry

    lax.fori_loop(0, 2 * NX // GROUPED, some_spans, 0)

    left = lax.broadcasted_iota(jnp.int32, (VD, 128), 1) < SPAN
    for p in range(HEADS // 2):
        tile = slice(p * 128, (p + 1) * 128)
        joined = jnp.concatenate([contexts[b, :LAT, tile] for b in range(2 * NX)], axis=1)
        both = jnp.dot(value_ref[p], joined, preferred_element_type=jnp.float32)
        for k in range(NX):
            early, late = [
                jnp.where(left, both[:VD, b * 128 : (b + 1) * 128], both[VD:, b * 128 : (b + 1) * 128])
                for b in (2 * k, 2 * k + 1)
            ]
            target = (x + NX - k) % NX
            for side, values in enumerate(
                (jnp.where(left, early, pltpu.roll(late, SPAN, axis=1)), jnp.where(left, pltpu.roll(early, SPAN, axis=1), late))
            ):
                out_ref[target, (2 * p + side) * VD : (2 * p + side + 1) * VD, :] = values.astype(jnp.bfloat16)
    for k in range(NX):
        logs = []
        for b in (2 * k, 2 * k + 1):
            rows = contexts[b, LAT:, :].astype(jnp.float32)
            rows = rows[:, :128] + rows[:, 128:]
            logs.append(rows + pltpu.roll(rows, SPAN, axis=1))
        out_ref[(x + NX - k) % NX, HEADS * VD :, :] = jnp.where(left[:16], *logs).astype(jnp.bfloat16)


def attend(spans, query, own, other, turned_value):
    return pl.pallas_call(
        attend_kernel,
        out_shape=jax.ShapeDtypeStruct((NX, PARTROWS, 2 * SPAN), jnp.bfloat16),
        in_specs=[SMEM] + [WHOLE] * 4,
        out_specs=WHOLE,
        scratch_shapes=[
            pltpu.VMEM((NSPAN * SPAN, ROWW), jnp.bfloat16),
            pltpu.VMEM((LAT, NSPAN * SPAN), jnp.bfloat16),
            pltpu.VMEM((2 * NX, LAT + 16, HEADS * SPAN), jnp.bfloat16),
            pltpu.SMEM((2 * NX,), jnp.int32),
        ],
        compiler_params=pltpu.CompilerParams(vmem_limit_bytes=VMEM_LIMIT),
    )(spans, query, own, other, turned_value)


def pack_kernel(keys_ref, out_ref):
    rows = keys_ref.shape[0]
    side = lax.broadcasted_iota(jnp.int32, (rows // 2, 128), 1) < ROPE
    tail = jnp.where(side, keys_ref[: rows // 2, LAT:], keys_ref[rows // 2 :, LAT:])
    for j in range(LAT // 128):
        out_ref[j * rows : (j + 1) * rows, :] = keys_ref[:, j * 128 : (j + 1) * 128]
    out_ref[LAT // 128 * rows :, :] = tail


def pack(keys):
    return pl.pallas_call(
        pack_kernel,
        out_shape=jax.ShapeDtypeStruct((keys.shape[0] * KEYW // 128, 128), jnp.bfloat16),
        in_specs=[WHOLE],
        out_specs=WHOLE,
        compiler_params=pltpu.CompilerParams(vmem_limit_bytes=VMEM_LIMIT),
    )(keys)


def add_kernel(first_ref, second_ref, out_ref):
    out_ref[...] = (first_ref[...].astype(jnp.float32) + second_ref[...].astype(jnp.float32)).astype(jnp.bfloat16)


def added(first, second):
    return pl.pallas_call(
        add_kernel,
        out_shape=jax.ShapeDtypeStruct(first.shape, jnp.bfloat16),
        in_specs=[WHOLE, WHOLE],
        out_specs=WHOLE,
        compiler_params=pltpu.CompilerParams(vmem_limit_bytes=VMEM_LIMIT),
    )(first, second)


def project_kernel(parts_ref, weight_ref, send_ref, keep_ref):
    c = lax.axis_index("c")
    heads = []
    packed = [parts_ref[i, HEADS * VD :, :].astype(jnp.float32) for i in range(NX)]
    for h in range(HEADS):
        logs = [(p[h : h + 1] + p[HEADS + h : HEADS + h + 1]) + p[2 * HEADS + h : 2 * HEADS + h + 1] for p in packed]
        highest = functools.reduce(jnp.maximum, logs)
        shares = [jnp.exp2(v - highest) for v in logs]
        inverse = 1.0 / functools.reduce(jnp.add, shares)
        merged = functools.reduce(
            jnp.add,
            [
                (shares[i] * inverse) * parts_ref[i, h * VD : (h + 1) * VD, :].astype(jnp.float32)
                for i in range(NX)
            ],
        )
        heads.append(merged.T.astype(jnp.bfloat16))
    head_out = jnp.concatenate(heads, axis=1)
    step = weight_ref.shape[1] // NY
    width = step // (NZH * NC)
    for y in range(NY):
        result = jnp.dot(
            head_out, weight_ref[:, y * step : (y + 1) * step], preferred_element_type=jnp.float32
        ).T.astype(jnp.bfloat16)
        for zh in range(NZH):
            even = result[2 * zh * width : (2 * zh + 1) * width]
            odd = result[(2 * zh + 1) * width : (2 * zh + 2) * width]
            keep_ref[y, zh] = jnp.where(c == 0, even, odd)
            send_ref[y, zh] = jnp.where(c == 0, odd, even)


def project(parts, weight):
    width = weight.shape[1] // (NY * NZH * NC)
    piece = jax.ShapeDtypeStruct((NY, NZH, width, 2 * SPAN), jnp.bfloat16)
    return pl.pallas_call(
        project_kernel,
        out_shape=(piece, piece),
        in_specs=[WHOLE, WHOLE],
        out_specs=(WHOLE, WHOLE),
        compiler_params=pltpu.CompilerParams(vmem_limit_bytes=VMEM_LIMIT),
    )(parts, weight)


def shifted(value, by):
    return lax.ppermute(value, "x", [(i, (i + by) % NX) for i in range(NX)])


def swapped(value, axis):
    return lax.ppermute(value, axis, [(0, 1), (1, 0)])


def exchanged(value, axis):
    return lax.all_to_all(value, axis, split_axis=0, concat_axis=0, tiled=True)


def on_device(query_plain, query_rotary, latent_keys, span_order, key_up, value_up, output_weight):
    zh = lax.axis_index("zh")
    tables = jnp.asarray(rotary_tables())
    sent_keys = pl.pallas_call(
        keys_kernel,
        out_shape=jax.ShapeDtypeStruct((GROUP, 8, ROWW), jnp.bfloat16),
        in_specs=[SMEM, WHOLE, WHOLE],
        out_specs=WHOLE,
    )(span_order, latent_keys, tables)
    rows = jax.ShapeDtypeStruct((2 * SPAN, QW), jnp.bfloat16)
    queries, kept_spans = pl.pallas_call(
        queries_kernel,
        out_shape=(rows, jax.ShapeDtypeStruct(span_order.shape, span_order.dtype)),
        in_specs=[SMEM, WHOLE, WHOLE, WHOLE, pl.BlockSpec(memory_space=pl.ANY)],
        out_specs=(WHOLE, SMEM),
    )(span_order, query_plain, query_rotary, tables, sent_keys)
    along_z = exchanged(sent_keys, ("zl", "zh")).reshape(GROUP * 8, ROWW)
    blocks = [queries, shifted(queries, 1), None, shifted(queries, NX - 1)]
    along_z, blocks[1], blocks[3] = lax.optimization_barrier((along_z, blocks[1], blocks[3]))
    blocks[2] = shifted(blocks[1], 1)
    own = lax.all_gather(pack(along_z), "y", axis=0, tiled=False)
    own, blocks[2] = lax.optimization_barrier((own, blocks[2]))
    other = swapped(own, "c")
    query, turned_value = absorb(blocks, key_up, value_up)
    parts = attend(kept_spans, query, own, other, turned_value)
    send, keep = project(exchanged(parts, "x"), output_weight)
    both = added(keep, swapped(send, "c"))
    over_y = exchanged(both, "y").astype(jnp.float32)
    mine = jnp.sum(lax.dynamic_index_in_dim(over_y, zh, 1, keepdims=False), axis=0)
    theirs = jnp.sum(lax.dynamic_index_in_dim(over_y, 1 - zh, 1, keepdims=False), axis=0).astype(jnp.bfloat16)
    return (mine + swapped(theirs, "zh").astype(jnp.float32)).astype(jnp.bfloat16).T


def solution(mesh):
    finer = Mesh(
        mesh.devices.reshape(NZL, NX, NY, NZH, NC), ("zl", "x", "y", "zh", "c")
    )
    in_specs = (
        P(CTX, TP),
        P(CTX, TP),
        P(CTX + TP, None),
        P(),
        P(TP, None, None),
        P(TP, None, None),
        P(TP, None),
    )
    return jax.shard_map(
        on_device, mesh=finer, in_specs=in_specs, out_specs=P(CTX, TP), check_vma=False
    )
```
